256 devices in a mesh: obj: 64 (over z, x, core), head: 4 (over y).
Axes of the slice: x: 4, y: 4, z: 8, core: 2. Of those that a mesh axis runs over, the one named last changes fastest.
Arguments:
- queries: bfloat16 [32768, 1024], P('obj', 'head'), may hold values from -120 to 120
- keys: bfloat16 [32768, 1024], P('obj', 'head'), may hold values from -10 to 10
- values: bfloat16 [32768, 1024], P('obj', 'head'), may hold values from -6 to 6
- camera: bfloat16 [128, 1024], P('obj', 'head'), may hold values from -4 to 4
- view_object: int32 [128], replicated, may hold values from 0 to 4, never falling along the last dimension, each value on 1 to 32 neighbouring positions
- out_weight: bfloat16 [1024, 1024], P('head'), may hold values from -0.1875 to 0.1875
Outputs:
- mixed: bfloat16 [32768, 1024], P(('obj', 'head'))
The draws below stay inside these ranges and needn't reach their ends.
Inputs may be any that keep to these rules, and one draw needn't show every extreme that they name: `view_object`: the view blocks of one object are consecutive and the object numbers never fall; an object has 1 to 32 views.
All inputs are finite; a program needn't handle non-finite values.
Results may differ from the reference program's by a relative error of at most 0.012.
Values may be sent and summed in bfloat16 or wider, within the bound.
No kernel may reach another device: no remote copies, remote signals or barrier semaphores. Data moves between devices by JAX's collectives and lax.ppermute only.
A program may use at most 128 MiB of HBM per device.

```python
import math
import jax
import jax.numpy as jnp
import numpy as np
from jax import lax

HEADS = 16
HD = 64
D = 1024
TOK_VIEW = 256
BLOCKS = 128
TOKENS = 32768
MOST_VIEWS = 32
OBJECTS = 5


def paired_draw(key):
    first, second = jax.random.split(jax.random.fold_in(key, 4101), 2)
    keys_f = jnp.clip(1.7 * jax.random.normal(first, (TOKENS, D), jnp.float32), -10.0, 10.0)
    queries_f = jnp.clip(1.7 * jax.random.normal(second, (TOKENS, D), jnp.float32), -10.0, 10.0)
    return (queries_f, keys_f)


def draw_queries(key, part):
    return paired_draw(key)[0].astype(jnp.bfloat16)


def draw_keys(key, part):
    return paired_draw(key)[1].astype(jnp.bfloat16)


def steps_of(rng, extent, shards, least, largest):
    level, own = 1.0, jax.random.fold_in(rng, 6)
    for position, parts in shards:
        draws = jnp.exp(jax.random.uniform(jax.random.fold_in(own, position), (parts,), jnp.float32, least / len(shards), largest / len(shards)))
        level = level * jnp.repeat(draws, extent[position] // parts).reshape([-1 if axis == position else 1 for axis in range(len(extent))])
    return level


def profile(number_of, total, reach, slope):
    weights = [(1 << 20) // math.isqrt(grade ** slope) + 1 for grade in range(2, number_of + 1)]
    spare, given = total - reach - (number_of - 1), [1] * (number_of - 1)
    while spare > 0:
        free = [i for i in range(number_of - 1) if given[i] < reach]
        whole, budget = sum([weights[i] for i in free]), spare
        for i in free:
            addition = min(reach - given[i], max(1, budget * weights[i] // whole), spare)
            given[i] = given[i] + addition
            spare = spare - addition
    return np.array([reach] + given)


def ragged_sizes(key, amount, total, limit, slope):
    if amount == 2:
        one = jax.random.randint(key, (), max(1, total - limit), min(limit, total - 1) + 1)
        return jnp.stack([one, total - one])
    sizes = jnp.asarray(profile(amount, total, limit, slope), jnp.int32)
    couples = (amount - 1) // 2
    giver, receiver = sizes[1:1 + 2 * couples:2], sizes[2:2 + 2 * couples:2]
    room = jnp.minimum(giver - 1, limit - receiver)
    moved = jax.random.randint(jax.random.fold_in(key, 1), (couples,), 0, 1 << 20) % (room + 1)
    sizes = sizes.at[1:1 + 2 * couples:2].set(giver - moved).at[2:2 + 2 * couples:2].set(receiver + moved)
    return sizes[jax.random.permutation(jax.random.fold_in(key, 2), amount)]


def bell_draw(key, dims, spread, bound, cuts=(), held_as=jnp.bfloat16):
    entries = spread * jax.random.normal(key, dims, jnp.float32)
    if cuts:
        entries = entries * steps_of(key, dims, cuts, -0.22, 0.18)
    return jnp.clip(entries, -bound, bound).astype(held_as)


def setup_inputs(seed: int = 0) -> dict:
    seeds = jax.random.split(jax.random.key(seed), 7)
    queries = draw_queries(jax.random.fold_in(seeds[6], 71), 0)
    keys = draw_keys(jax.random.fold_in(seeds[6], 71), 0)
    values = bell_draw(seeds[2], (TOKENS, D), 1.0, 6.0, ((0, 64), (1, 4)))
    camera = bell_draw(seeds[3], (BLOCKS, D), 0.7, 4.0, ((0, 64), (1, 4)))
    view_object = jnp.searchsorted(jnp.cumsum(ragged_sizes(seeds[4], OBJECTS, BLOCKS, MOST_VIEWS, 2)), jnp.arange(BLOCKS), side="right").astype(jnp.int32)
    out_weight = bell_draw(seeds[5], (D, D), D ** -0.5, 0.1875, ((0, 4),))
    return {"queries": queries, "keys": keys, "values": values, "camera": camera, "view_object": view_object, "out_weight": out_weight}


def reference(queries, keys, values, camera, view_object, out_weight):
    span = MOST_VIEWS - 1
    window = 2 * span + 1
    scale = 1.0 / math.sqrt(HD)
    cam_tok = jnp.repeat(camera.astype(jnp.float32), TOK_VIEW, axis=0)
    query_c = (queries.astype(jnp.float32) + cam_tok).astype(jnp.bfloat16)
    key_c = (keys.astype(jnp.float32) + cam_tok).astype(jnp.bfloat16)
    query_blocks = query_c.reshape(BLOCKS, TOK_VIEW, HEADS, HD)
    key_blocks = key_c.reshape(BLOCKS, TOK_VIEW, HEADS, HD)
    value_blocks = values.reshape(BLOCKS, TOK_VIEW, HEADS, HD)
    zero_blocks = jnp.zeros((span, TOK_VIEW, HEADS, HD), jnp.bfloat16)
    key_padded = jnp.concatenate([zero_blocks, key_blocks, zero_blocks], axis=0)
    value_padded = jnp.concatenate([zero_blocks, value_blocks, zero_blocks], axis=0)
    none_ids = jnp.full((span,), -1, jnp.int32)
    ids_padded = jnp.concatenate([none_ids, view_object.astype(jnp.int32), none_ids], axis=0)

    def attend_block(block_index):
        key_window = lax.dynamic_slice_in_dim(key_padded, block_index, window, 0).reshape(window * TOK_VIEW, HEADS, HD)
        value_window = lax.dynamic_slice_in_dim(value_padded, block_index, window, 0).reshape(window * TOK_VIEW, HEADS, HD)
        id_window = lax.dynamic_slice_in_dim(ids_padded, block_index, window, 0)
        query_block = lax.dynamic_index_in_dim(query_blocks, block_index, 0, keepdims=False)
        scores = jnp.einsum('qhd,khd->hqk', query_block.astype(jnp.float32), key_window.astype(jnp.float32)) * scale
        own_object = lax.dynamic_index_in_dim(view_object.astype(jnp.int32), block_index, 0, keepdims=False)
        allowed = jnp.repeat(id_window, TOK_VIEW) == own_object
        scores = jnp.where(allowed[None, None, :], scores, -jnp.inf)
        row_max = lax.optimization_barrier(jnp.max(scores, axis=-1, keepdims=True))
        weights = jnp.exp(scores - row_max)
        row_sum = lax.optimization_barrier(jnp.sum(weights, axis=-1))
        rounded = lax.optimization_barrier(weights.astype(jnp.bfloat16)).astype(jnp.float32)
        summed = jnp.einsum('hqk,khd->qhd', rounded, value_window.astype(jnp.float32))
        attended = summed / jnp.transpose(row_sum)[:, :, None]
        return attended.reshape(TOK_VIEW, HEADS * HD).astype(jnp.bfloat16)
    attended = lax.map(attend_block, jnp.arange(BLOCKS, dtype=jnp.int32)).reshape(TOKENS, HEADS * HD)
    return jnp.dot(attended, out_weight, preferred_element_type=jnp.float32).astype(jnp.bfloat16)
```

```python
import functools
import math

import jax
import jax.numpy as jnp
from jax import lax
from jax.experimental import pallas as pl
from jax.experimental.pallas import tpu as pltpu
from jax.sharding import Mesh, PartitionSpec as P

HD = 64
TOK_VIEW = 256
X = 4
C = 2
PLANE = 16
LOCAL = 8
LANES = 128
BASE2 = math.log2(math.e) / math.sqrt(HD)
NEG = -1e30
VMEM_BYTES = 56 << 20


def swap_halves(x):
    return jnp.concatenate([x[:, HD:], x[:, :HD]], axis=1)


def low_lanes(shape):
    return lax.broadcasted_iota(jnp.int32, shape, 1) < HD


def pack_kernel(q_ref, k_ref, v_ref, cam_ref, kv_ref, qp_ref):
    cam = cam_ref[...].astype(jnp.float32)
    low = low_lanes((TOK_VIEW, LANES))
    for pair in range(2):
        cols = slice(pair * LANES, (pair + 1) * LANES)
        queries = []
        for view in range(2):
            rows = slice(view * TOK_VIEW, (view + 1) * TOK_VIEW)
            shift = cam[view : view + 1, cols]
            k = k_ref[rows, cols].astype(jnp.float32) + shift
            v = v_ref[rows, cols].astype(jnp.float32)
            kv_ref[2 * pair, rows, :] = jnp.where(low, k, swap_halves(v)).astype(jnp.bfloat16)
            kv_ref[2 * pair + 1, rows, :] = jnp.where(low, swap_halves(k), v).astype(jnp.bfloat16)
            queries.append(q_ref[rows, cols].astype(jnp.float32) + shift)
        first, second = queries
        qp_ref[2 * pair] = jnp.where(low, first, swap_halves(second)).astype(jnp.bfloat16)
        qp_ref[2 * pair + 1] = jnp.where(low, swap_halves(first), second).astype(jnp.bfloat16)


def attend_kernel(bounds, q_own, q_oth, *refs, planes, has_state):
    kv_hbm = refs[:planes]
    refs = refs[planes:]
    if has_state:
        state_ref, refs = refs[0], refs[1:]
    out_ref, kv_buf, v_buf, sems = refs
    copies = [pltpu.make_async_copy(kv_hbm[p], kv_buf.at[p], sems.at[p]) for p in range(planes)]
    for copy in copies:
        copy.start()
    if not has_state:
        lane = lax.broadcasted_iota(jnp.int32, (TOK_VIEW, LANES), 1)
        blank = jnp.where(lane < HD // 2, NEG, 0.0)
    for p in range(planes):
        copies[p].wait()
        low = low_lanes((2048, LANES))
        v_buf[p] = jnp.where(low, jnp.ones((), jnp.bfloat16), kv_buf[p])

    def process(rows, row0, q, p, start, count):
        here = pl.ds(row0, rows)

        def variant(n):
            keys = pl.ds(pl.multiple_of(start * TOK_VIEW, TOK_VIEW), n * TOK_VIEW)
            state = out_ref[here, :]
            old = state[:, :1]
            s = lax.dot_general(
                q,
                kv_buf[p, keys, :],
                (((1,), (1,)), ((), ())),
                preferred_element_type=jnp.float32,
            )
            new = jnp.maximum(old, jnp.max(s, axis=1, keepdims=True))
            weights = jnp.exp2(s * BASE2 - new * BASE2).astype(jnp.bfloat16)
            factor = jnp.exp2((old - new) * BASE2)
            update = jnp.dot(weights, v_buf[p, keys, :], preferred_element_type=jnp.float32)
            lane = lax.broadcasted_iota(jnp.int32, (rows, LANES), 1)
            out_ref[here, :] = jnp.where(lane < HD // 2, new, state * factor + update)

        for n in range(1, LOCAL + 1):
            pl.when(count == n)(functools.partial(variant, n))

    def tile(t, carry):
        row0 = pl.multiple_of(t * 2 * TOK_VIEW, 2 * TOK_VIEW)
        rows = pl.ds(row0, 2 * TOK_VIEW)
        if has_state:
            out_ref[rows, :] = state_ref[rows, :]
        else:
            out_ref[pl.ds(row0, TOK_VIEW), :] = blank
            out_ref[pl.ds(row0 + TOK_VIEW, TOK_VIEW), :] = blank
        packed = jnp.where(t < X, q_own[t % X], q_oth[t % X])
        low = low_lanes((TOK_VIEW, LANES))
        zero = jnp.zeros((), jnp.bfloat16)
        first = jnp.where(low, packed, zero)
        second = jnp.where(low, swap_halves(packed), zero)

        def plane(p, carry):
            at = ((p * 2 * X + t) * 2) * 2
            start0, end0 = bounds[at], bounds[at + 1]
            start1, end1 = bounds[at + 2], bounds[at + 3]
            alike = jnp.logical_and(start0 == start1, end0 == end1)

            @pl.when(alike)
            def _():
                q = jnp.concatenate([first, second], axis=0)
                process(2 * TOK_VIEW, row0, q, p, start0, end0 - start0)

            @pl.when(jnp.logical_not(alike))
            def _():
                def one(w, carry):
                    q = jnp.where(w == 0, first, second)
                    start = jnp.where(w == 0, start0, start1)
                    end = jnp.where(w == 0, end0, end1)
                    process(
                        TOK_VIEW,
                        pl.multiple_of(row0 + w * TOK_VIEW, TOK_VIEW),
                        q,
                        p,
                        start,
                        end - start,
                    )
                    return carry

                lax.fori_loop(0, 2, one, 0)

            return carry

        lax.fori_loop(0, planes, plane, 0)
        return carry

    lax.fori_loop(0, 2 * X, tile, 0)


def attend(bounds, q_own, q_oth, kv_planes, state):
    planes = len(kv_planes)
    vmem = pl.BlockSpec(memory_space=pltpu.VMEM)
    inputs = [bounds, q_own, q_oth, *kv_planes] + ([] if state is None else [state])
    specs = [pl.BlockSpec(memory_space=pltpu.SMEM), vmem, vmem]
    specs += [pl.BlockSpec(memory_space=pl.ANY)] * planes + ([] if state is None else [vmem])
    return pl.pallas_call(
        functools.partial(attend_kernel, planes=planes, has_state=state is not None),
        out_shape=jax.ShapeDtypeStruct((2 * X * 2 * TOK_VIEW, LANES), jnp.float32),
        in_specs=specs,
        out_specs=vmem,
        scratch_shapes=[
            pltpu.VMEM((planes, LOCAL * TOK_VIEW, LANES), jnp.bfloat16),
            pltpu.VMEM((planes, LOCAL * TOK_VIEW, LANES), jnp.bfloat16),
            pltpu.SemaphoreType.DMA((planes,)),
        ],
        compiler_params=pltpu.CompilerParams(vmem_limit_bytes=VMEM_BYTES),
        name=f"attend_{planes}",
    )(*inputs)


def join_kernel(own_ref, got_ref, out_ref):
    def step(i, carry):
        rows = pl.ds(pl.multiple_of(i * LANES, LANES), LANES)
        a, b = own_ref[rows, :], got_ref[rows, :]
        m_a, m_b = a[:, :1], b[:, :1]
        top = jnp.maximum(m_a, m_b)
        total = a * jnp.exp2((m_a - top) * BASE2) + b * jnp.exp2((m_b - top) * BASE2)
        done = total / total[:, HD // 2 : HD // 2 + 1]
        upper, lower = done[:HD], done[HD:]
        out_ref[i] = jnp.where(low_lanes((HD, LANES)), swap_halves(upper), lower).astype(
            jnp.bfloat16
        )
        return carry

    lax.fori_loop(0, 16, step, 0)


def project_kernel(parts_ref, weight_ref, out_ref, rows_ref):
    low = low_lanes((HD, LANES))
    for pair in range(8):
        even, odd = 2 * pair, 2 * pair + 1
        a = parts_ref[(even % 4) * 4 + even // 4].astype(jnp.float32)
        b = parts_ref[(odd % 4) * 4 + odd // 4].astype(jnp.float32)
        cols = slice(pair * LANES, (pair + 1) * LANES)
        rows_ref[:HD, cols] = jnp.where(low, a, swap_halves(b)).astype(jnp.bfloat16)
        rows_ref[HD:, cols] = jnp.where(low, swap_halves(a), b).astype(jnp.bfloat16)
    out_ref[...] = jnp.dot(
        rows_ref[...], weight_ref[...], preferred_element_type=jnp.float32
    ).astype(jnp.bfloat16)


def key_ranges(view_object, plane, core):
    tile = jnp.arange(2 * X)
    inner = 4 * (tile % X) + 2 * jnp.where(tile < X, core, 1 - core)
    view = PLANE * plane + inner[:, None] + jnp.arange(2)[None, :]
    own = jnp.sum(
        jnp.where(
            jnp.arange(view_object.shape[0])[None, None, :] == view[:, :, None],
            view_object[None, None, :],
            0,
        ),
        axis=-1,
    )
    first = jnp.sum(view_object[None, None, :] < own[:, :, None], axis=-1)
    end = jnp.sum(view_object[None, None, :] <= own[:, :, None], axis=-1)
    edges = jnp.stack([first, end], axis=-1)
    offset = PLANE * (plane + jnp.arange(-2, 3))
    edges = jnp.clip(edges[None] - offset[:, None, None, None], 0, PLANE)
    local = 2 * (edges // 4) + jnp.clip(edges % 4 - 2 * core, 0, 2)
    return local.astype(jnp.int32).reshape(5, -1)


def body(queries, keys, values, camera, view_object, out_weight):
    vmem = pl.BlockSpec(memory_space=pltpu.VMEM)
    z_count = lax.axis_size("z")
    up = [(i, (i + 1) % z_count) for i in range(z_count)]
    down = [(i, (i - 1) % z_count) for i in range(z_count)]
    cores = [(0, 1), (1, 0)]
    plane, core = lax.axis_index("z"), lax.axis_index("c")
    ranges = key_ranges(view_object, plane, core)
    weight = lax.all_gather(out_weight, "y", axis=0, tiled=True)

    kv_send, q_send = pl.pallas_call(
        pack_kernel,
        out_shape=(
            jax.ShapeDtypeStruct((X, 2 * TOK_VIEW, LANES), jnp.bfloat16),
            jax.ShapeDtypeStruct((X, TOK_VIEW, LANES), jnp.bfloat16),
        ),
        in_specs=[vmem] * 4,
        out_specs=(vmem, vmem),
        compiler_params=pltpu.CompilerParams(vmem_limit_bytes=VMEM_BYTES),
        name="pack",
    )(queries, keys, values, camera)
    kv = lax.all_to_all(kv_send, "x", 0, 0, tiled=True).reshape(-1, LANES)
    below = lax.ppermute(kv, "z", up)
    above = lax.ppermute(kv, "z", down)
    q_own = lax.all_to_all(q_send, "x", 0, 0, tiled=True)
    q_oth = lax.ppermute(q_own, "c", cores)
    state = attend(ranges[2], q_own, q_oth, [kv], None)
    below_far = lax.ppermute(below, "z", up)
    above_far = lax.ppermute(above, "z", down)
    near = jnp.concatenate([ranges[1], ranges[3]])
    state = attend(near, q_own, q_oth, [below, above], state)
    far = jnp.concatenate([ranges[0], ranges[4]])
    state = attend(far, q_own, q_oth, [below_far, above_far], state)
    half = state.shape[0] // 2
    got = lax.ppermute(state[half:], "c", cores)
    attended = pl.pallas_call(
        join_kernel,
        out_shape=jax.ShapeDtypeStruct((16, HD, LANES), jnp.bfloat16),
        in_specs=[vmem, vmem],
        out_specs=vmem,
        compiler_params=pltpu.CompilerParams(vmem_limit_bytes=VMEM_BYTES),
        name="join",
    )(state[:half], got)
    parts = lax.all_to_all(attended, ("x", "y"), 0, 0, tiled=True)
    return pl.pallas_call(
        project_kernel,
        out_shape=jax.ShapeDtypeStruct((LANES, 1024), jnp.bfloat16),
        in_specs=[vmem, vmem],
        out_specs=vmem,
        scratch_shapes=[pltpu.VMEM((LANES, 1024), jnp.bfloat16)],
        compiler_params=pltpu.CompilerParams(vmem_limit_bytes=VMEM_BYTES),
        name="project",
    )(parts, weight)


def solution(mesh):
    views = mesh.shape["obj"] // (X * C)
    grid = Mesh(mesh.devices.reshape(views, X, C, mesh.shape["head"]), ("z", "x", "c", "y"))
    obj = ("z", "x", "c")
    return jax.shard_map(
        body,
        mesh=grid,
        in_specs=(
            P(obj, "y"),
            P(obj, "y"),
            P(obj, "y"),
            P(obj, "y"),
            P(),
            P("y", None),
        ),
        out_specs=P((*obj, "y"), None),
        check_vma=False,
    )
```

```python
import functools
import math

import jax
import jax.numpy as jnp
from jax import lax
from jax.experimental import pallas as pl
from jax.experimental.pallas import tpu as pltpu
from jax.sharding import Mesh, PartitionSpec as P

HD = 64
TOK_VIEW = 256
X = 4
C = 2
PLANE = 16
LOCAL = 8
LANES = 128
BASE2 = math.log2(math.e) / math.sqrt(HD)
NEG = -1e30
VMEM_BYTES = 56 << 20


def swap_halves(x):
    return jnp.concatenate([x[:, HD:], x[:, :HD]], axis=1)


def low_lanes(shape):
    return lax.broadcasted_iota(jnp.int32, shape, 1) < HD


def pack_kernel(q_ref, k_ref, v_ref, cam_ref, out_ref):
    cam = cam_ref[...].astype(jnp.float32)
    low = low_lanes((TOK_VIEW, LANES))
    for pair in range(2):
        cols = slice(pair * LANES, (pair + 1) * LANES)
        queries = []
        for view in range(2):
            rows = slice(view * TOK_VIEW, (view + 1) * TOK_VIEW)
            shift = cam[view : view + 1, cols]
            k = k_ref[rows, cols].astype(jnp.float32) + shift
            v = v_ref[rows, cols].astype(jnp.float32)
            out_ref[2 * pair, rows, :] = jnp.where(low, k, swap_halves(v)).astype(jnp.bfloat16)
            out_ref[2 * pair + 1, rows, :] = jnp.where(low, swap_halves(k), v).astype(jnp.bfloat16)
            queries.append(q_ref[rows, cols].astype(jnp.float32) + shift)
        first, second = queries
        rows = slice(2 * TOK_VIEW, 3 * TOK_VIEW)
        out_ref[2 * pair, rows, :] = jnp.where(low, first, swap_halves(second)).astype(jnp.bfloat16)
        out_ref[2 * pair + 1, rows, :] = jnp.where(low, swap_halves(first), second).astype(
            jnp.bfloat16
        )


def by_count(count, low, high, variant):
    if low == high:
        pl.when(count == low)(functools.partial(variant, low))
        return
    middle = (low + high) // 2
    pl.when(count <= middle)(lambda: by_count(count, low, middle, variant))
    pl.when(count > middle)(lambda: by_count(count, middle + 1, high, variant))


def attend_kernel(bounds, q_ref, *refs, sides, side0, tile0, has_state):
    planes = sum(sides)
    kv_hbm = refs[:planes]
    refs = refs[planes:]
    if has_state:
        state_ref, refs = refs[0], refs[1:]
    out_ref, kv_buf, v_buf, sems = refs
    t = pl.program_id(0)

    @pl.when(t == 0)
    def _():
        size = LOCAL * TOK_VIEW
        copies = [
            pltpu.make_async_copy(kv_hbm[p], kv_buf.at[pl.ds(p * size, size), :], sems.at[p])
            for p in range(planes)
        ]
        for copy in copies:
            copy.start()
        for p in range(planes):
            copies[p].wait()
            part = pl.ds(p * size, size)
            v_buf[part, :] = jnp.where(
                low_lanes((size, LANES)), jnp.ones((), jnp.bfloat16), kv_buf[part, :]
            )

    if has_state:
        out_ref[...] = state_ref[...]
    else:
        lane = lax.broadcasted_iota(jnp.int32, (2 * TOK_VIEW, LANES), 1)
        out_ref[...] = jnp.where(lane < HD // 2, NEG, 0.0)
    packed = q_ref[0]
    low = low_lanes((TOK_VIEW, LANES))
    zero = jnp.zeros((), jnp.bfloat16)
    first = jnp.where(low, packed, zero)
    second = jnp.where(low, swap_halves(packed), zero)
    both = jnp.concatenate([first, second], axis=0)

    def process(rows, row0, q, start, count):
        here = pl.ds(row0, rows)

        def variant(n):
            keys = pl.ds(pl.multiple_of(start * TOK_VIEW, TOK_VIEW), n * TOK_VIEW)
            state = out_ref[here, :]
            old = state[:, :1]
            s = lax.dot_general(
                q, kv_buf[keys, :], (((1,), (1,)), ((), ())), preferred_element_type=jnp.float32
            )
            new = jnp.maximum(old, jnp.max(s, axis=1, keepdims=True))
            weights = jnp.exp2(s * BASE2 - new * BASE2).astype(jnp.bfloat16)
            factor = jnp.exp2((old - new) * BASE2)
            update = jnp.dot(weights, v_buf[keys, :], preferred_element_type=jnp.float32)
            lane = lax.broadcasted_iota(jnp.int32, (rows, LANES), 1)
            out_ref[here, :] = jnp.where(lane < HD // 2, new, state * factor + update)

        by_count(count, 1, LOCAL, variant)

    def visit(rows, row0, q, start, end):
        def chunk(i, carry):
            process(rows, row0, q, start + LOCAL * i, jnp.minimum(end - start - LOCAL * i, LOCAL))
            return carry

        lax.fori_loop(0, (end - start + LOCAL - 1) // LOCAL, chunk, 0)

    def side(i, carry):
        at = (((side0 + 2 * i) * 2 * X + tile0 + t) * 2) * 2
        shift = LOCAL * sides[0] * i
        start0, end0 = bounds[at] + shift, bounds[at + 1] + shift
        start1, end1 = bounds[at + 2] + shift, bounds[at + 3] + shift
        alike = jnp.logical_and(start0 == start1, end0 == end1)

        @pl.when(alike)
        def _():
            visit(2 * TOK_VIEW, 0, both, start0, end0)

        @pl.when(jnp.logical_not(alike))
        def _():
            def one(w, carry):
                visit(
                    TOK_VIEW,
                    pl.multiple_of(w * TOK_VIEW, TOK_VIEW),
                    jnp.where(w == 0, first, second),
                    jnp.where(w == 0, start0, start1),
                    jnp.where(w == 0, end0, end1),
                )
                return carry

            lax.fori_loop(0, 2, one, 0)

        return carry

    lax.fori_loop(0, len(sides), side, 0)


def attend(bounds, q, q_row, tile0, kv_planes, sides, side0, state, name):
    planes = len(kv_planes)
    block = pl.BlockSpec((2 * TOK_VIEW, LANES), lambda t: (t, 0))
    inputs = [bounds, q, *kv_planes] + ([] if state is None else [state])
    specs = [
        pl.BlockSpec(memory_space=pltpu.SMEM),
        pl.BlockSpec((1, TOK_VIEW, LANES), lambda t: (t, q_row, 0)),
    ]
    specs += [pl.BlockSpec(memory_space=pl.ANY)] * planes + ([] if state is None else [block])
    return pl.pallas_call(
        functools.partial(
            attend_kernel, sides=sides, side0=side0, tile0=tile0, has_state=state is not None
        ),
        grid=(X,),
        out_shape=jax.ShapeDtypeStruct((X * 2 * TOK_VIEW, LANES), jnp.float32),
        in_specs=specs,
        out_specs=block,
        scratch_shapes=[
            pltpu.VMEM((planes * LOCAL * TOK_VIEW, LANES), jnp.bfloat16),
            pltpu.VMEM((planes * LOCAL * TOK_VIEW, LANES), jnp.bfloat16),
            pltpu.SemaphoreType.DMA((planes,)),
        ],
        compiler_params=pltpu.CompilerParams(vmem_limit_bytes=VMEM_BYTES),
        cost_estimate=pl.CostEstimate(
            flops=planes * 2 * (X * 2 * TOK_VIEW) * (LOCAL * TOK_VIEW) * 2 * TOK_VIEW,
            transcendentals=planes * (X * 2 * TOK_VIEW) * (LOCAL * TOK_VIEW),
            bytes_accessed=planes << 20,
        ),
        name=name,
    )(*inputs)


def join_kernel(own_ref, got_ref, out_ref):
    a, b = own_ref[...], got_ref[...]
    m_a, m_b = a[:, :1], b[:, :1]
    top = jnp.maximum(m_a, m_b)
    total = a * jnp.exp2((m_a - top) * BASE2) + b * jnp.exp2((m_b - top) * BASE2)
    done = total * (1.0 / total[:, HD // 2 : HD // 2 + 1])
    low = low_lanes((HD, LANES))
    for i in range(4):
        upper = done[i * LANES : i * LANES + HD]
        lower = done[i * LANES + HD : (i + 1) * LANES]
        out_ref[i] = jnp.where(low, swap_halves(upper), lower).astype(jnp.bfloat16)


def project_kernel(y_ref, parts_ref, *refs):
    weights, (out_ref, rows_ref, sum_ref) = refs[:4], refs[4:]
    low = low_lanes((HD, LANES))
    for k in range(4):
        y = (y_ref[0] + 4 - k) % 4
        for pair in range(2):
            a = parts_ref[2 * pair * 4 + y].astype(jnp.float32)
            b = parts_ref[(2 * pair + 1) * 4 + y].astype(jnp.float32)
            cols = slice(pair * LANES, (pair + 1) * LANES)
            rows_ref[k, :HD, cols] = jnp.where(low, a, swap_halves(b)).astype(jnp.bfloat16)
            rows_ref[k, HD:, cols] = jnp.where(low, swap_halves(a), b).astype(jnp.bfloat16)
    for k in range(4):
        part = jnp.dot(rows_ref[k], weights[k][...], preferred_element_type=jnp.float32)
        if k == 0:
            sum_ref[...] = part
        elif k < 3:
            sum_ref[...] += part
        else:
            out_ref[...] = (sum_ref[...] + part).astype(jnp.bfloat16)


def key_ranges(view_object, plane, core):
    tile = jnp.arange(2 * X)
    inner = 4 * (tile % X) + 2 * jnp.where(tile < X, core, 1 - core)
    view = PLANE * plane + inner[:, None] + jnp.arange(2)[None, :]
    own = jnp.sum(
        jnp.where(
            jnp.arange(view_object.shape[0])[None, None, :] == view[:, :, None],
            view_object[None, None, :],
            0,
        ),
        axis=-1,
    )
    first = jnp.sum(view_object[None, None, :] < own[:, :, None], axis=-1)
    end = jnp.sum(view_object[None, None, :] <= own[:, :, None], axis=-1)
    edges = jnp.stack([first, end], axis=-1)
    offset = PLANE * (plane + jnp.array([-2, 0, 1]))
    most = PLANE * jnp.array([2, 1, 2])
    edges = jnp.clip(edges[None] - offset[:, None, None, None], 0, most[:, None, None, None])
    local = 2 * (edges // 4) + jnp.clip(edges % 4 - 2 * core, 0, 2)
    return local.astype(jnp.int32).reshape(-1)


def body(queries, keys, values, camera, view_object, out_weight):
    vmem = pl.BlockSpec(memory_space=pltpu.VMEM)
    z_count = lax.axis_size("z")
    up = [(i, (i + 1) % z_count) for i in range(z_count)]
    down = [(i, (i - 1) % z_count) for i in range(z_count)]
    cores = [(0, 1), (1, 0)]
    plane, core = lax.axis_index("z"), lax.axis_index("c")
    sent = pl.pallas_call(
        pack_kernel,
        out_shape=jax.ShapeDtypeStruct((X, 3 * TOK_VIEW, LANES), jnp.bfloat16),
        in_specs=[vmem] * 4,
        out_specs=vmem,
        compiler_params=pltpu.CompilerParams(vmem_limit_bytes=VMEM_BYTES),
        name="pack",
    )(queries, keys, values, camera)
    ours = lax.all_to_all(sent, "x", 0, 0, tiled=True)
    bounds = key_ranges(view_object, plane, core)
    kv = ours[:, : 2 * TOK_VIEW].reshape(-1, LANES)
    below = lax.ppermute(kv, "z", up)
    above = lax.ppermute(kv, "z", down)
    q_oth = lax.ppermute(ours[:, 2 * TOK_VIEW :], "c", cores)
    weights = [out_weight] + [
        lax.ppermute(out_weight, "y", [(i, (i + k) % 4) for i in range(4)]) for k in (1, 2, 3)
    ]
    own = attend(bounds, ours, 2, 0, [kv], (1,), 1, None, "here_own")
    below, above, own = lax.optimization_barrier((below, above, own))
    below_far = lax.ppermute(below, "z", up)
    above_far = lax.ppermute(above, "z", down)
    oth = attend(bounds, q_oth, 0, X, [kv], (1,), 1, None, "here_other")
    rest = [below_far, below, above, above_far]
    oth = attend(bounds, q_oth, 0, X, rest, (2, 2), 0, oth, "rest_other")
    got = lax.ppermute(oth, "c", cores)
    own = attend(bounds, ours, 2, 0, rest, (2, 2), 0, own, "rest_own")
    state_block = pl.BlockSpec((2 * TOK_VIEW, LANES), lambda t: (t, 0))
    attended = pl.pallas_call(
        join_kernel,
        grid=(X,),
        out_shape=jax.ShapeDtypeStruct((16, HD, LANES), jnp.bfloat16),
        in_specs=[state_block, state_block],
        out_specs=pl.BlockSpec((4, HD, LANES), lambda t: (t, 0, 0)),
        compiler_params=pltpu.CompilerParams(vmem_limit_bytes=VMEM_BYTES),
        name="join",
    )(own, got)
    parts = lax.all_to_all(attended, ("x", "y"), 0, 0, tiled=True)
    return pl.pallas_call(
        project_kernel,
        out_shape=jax.ShapeDtypeStruct((LANES, 1024), jnp.bfloat16),
        in_specs=[pl.BlockSpec(memory_space=pltpu.SMEM)] + [vmem] * 5,
        out_specs=vmem,
        scratch_shapes=[
            pltpu.VMEM((4, LANES, 256), jnp.bfloat16),
            pltpu.VMEM((LANES, 1024), jnp.float32),
        ],
        compiler_params=pltpu.CompilerParams(vmem_limit_bytes=VMEM_BYTES),
        name="project",
    )(lax.axis_index("y").astype(jnp.int32).reshape(1), parts, *weights)


def solution(mesh):
    views = mesh.shape["obj"] // (X * C)
    grid = Mesh(mesh.devices.reshape(views, X, C, mesh.shape["head"]), ("z", "x", "c", "y"))
    obj = ("z", "x", "c")
    return jax.shard_map(
        body,
        mesh=grid,
        in_specs=(
            P(obj, "y"),
            P(obj, "y"),
            P(obj, "y"),
            P(obj, "y"),
            P(),
            P("y", None),
        ),
        out_specs=P((*obj, "y"), None),
        check_vma=False,
    )
```

```python
import functools
import math

import jax
import jax.numpy as jnp
from jax import lax
from jax.experimental import pallas as pl
from jax.experimental.pallas import tpu as pltpu
from jax.sharding import Mesh, PartitionSpec as P

HD = 64
TOK_VIEW = 256
X = 4
C = 2
PLANE = 16
LOCAL = 8
LANES = 128
BASE2 = math.log2(math.e) / math.sqrt(HD)
NEG = -1e30
VMEM_BYTES = 56 << 20


def swap_halves(x):
    return jnp.concatenate([x[:, HD:], x[:, :HD]], axis=1)


def low_lanes(shape):
    return lax.broadcasted_iota(jnp.int32, shape, 1) < HD


def pack_kernel(q_ref, k_ref, v_ref, cam_ref, out_ref):
    cam = cam_ref[...].astype(jnp.float32)
    low = low_lanes((TOK_VIEW, LANES))
    for pair in range(2):
        cols = slice(pair * LANES, (pair + 1) * LANES)
        queries = []
        for view in range(2):
            rows = slice(view * TOK_VIEW, (view + 1) * TOK_VIEW)
            shift = cam[view : view + 1, cols]
            k = k_ref[rows, cols].astype(jnp.float32) + shift
            v = v_ref[rows, cols].astype(jnp.float32)
            out_ref[2 * pair, rows, :] = jnp.where(low, k, swap_halves(v)).astype(jnp.bfloat16)
            out_ref[2 * pair + 1, rows, :] = jnp.where(low, swap_halves(k), v).astype(jnp.bfloat16)
            queries.append(q_ref[rows, cols].astype(jnp.float32) + shift)
        first, second = queries
        rows = slice(2 * TOK_VIEW, 3 * TOK_VIEW)
        out_ref[2 * pair, rows, :] = jnp.where(low, first, swap_halves(second)).astype(jnp.bfloat16)
        out_ref[2 * pair + 1, rows, :] = jnp.where(low, swap_halves(first), second).astype(
            jnp.bfloat16
        )


def attend_kernel(bounds_hbm, q_hbm, *refs, sides, side0, tile0, q_row, has_state):
    planes = sum(sides)
    kv_hbm = refs[:planes]
    refs = refs[planes:]
    if has_state:
        state_hbm, refs = refs[0], refs[1:]
    out_hbm, bounds, bounds_sem, q_buf, q_rows, kv_buf, v_buf, state, top, kv_sems, q_sem, in_sems, out_sems = refs
    size, rows_tile = LOCAL * TOK_VIEW, 2 * TOK_VIEW
    kv_copies = [
        pltpu.make_async_copy(kv_hbm[p], kv_buf.at[pl.ds(p * size, size), :], kv_sems.at[p])
        for p in range(planes)
    ]
    q_copy = pltpu.make_async_copy(q_hbm.at[:, pl.ds(q_row, TOK_VIEW), :], q_buf, q_sem)

    def rows_of(t):
        return pl.ds(pl.multiple_of(t * rows_tile, rows_tile), rows_tile)

    def state_in(t):
        return pltpu.make_async_copy(
            state_hbm.at[rows_of(t), :], state.at[rows_of(t), :], in_sems.at[t]
        )

    def state_out(t):
        return pltpu.make_async_copy(
            state.at[rows_of(t), :], out_hbm.at[rows_of(t), :], out_sems.at[t]
        )

    bounds_copy = pltpu.make_async_copy(bounds_hbm, bounds, bounds_sem)
    bounds_copy.start()
    q_copy.start()
    if has_state:
        for t in range(X):
            state_in(t).start()
    for copy in kv_copies:
        copy.start()
    lane = lax.broadcasted_iota(jnp.int32, (1, LANES), 1)
    keep = jnp.where(lane < HD, 0.0, 1.0).astype(jnp.bfloat16)
    ones = jnp.where(lane < HD, 1.0, 0.0).astype(jnp.bfloat16)

    def plane_ready(first, end):
        for p in range(first, end):
            kv_copies[p].wait()

        def fill(i, carry):
            part = pl.ds(pl.multiple_of(i * 2 * TOK_VIEW, 2 * TOK_VIEW), 2 * TOK_VIEW)
            v_buf[part, :] = kv_buf[part, :] * keep + ones
            return carry

        lax.fori_loop(first * LOCAL // 2, end * LOCAL // 2, fill, 0)

    q_copy.wait()
    for t in range(X):
        packed = q_buf[t]
        low = low_lanes((TOK_VIEW, LANES))
        zero = jnp.zeros((), jnp.bfloat16)
        row = t * rows_tile
        q_rows[row : row + TOK_VIEW, :] = jnp.where(low, packed, zero)
        q_rows[row + TOK_VIEW : row + rows_tile, :] = jnp.where(low, swap_halves(packed), zero)
        if has_state:
            state_in(t).wait()
            packed = state[row : row + rows_tile, :]
            top[row : row + rows_tile, :] = jnp.broadcast_to(packed[:, :1], packed.shape)
        else:
            top[row : row + rows_tile, :] = jnp.full((rows_tile, LANES), NEG, jnp.float32)
            state[row : row + rows_tile, :] = jnp.zeros((rows_tile, LANES), jnp.float32)

    def visit(rows, row0, tiles, start, end):
        def variant(n, key0):
            keys = pl.ds(pl.multiple_of(key0 * TOK_VIEW, TOK_VIEW), n * TOK_VIEW)

            def step(i, carry):
                here = pl.ds(pl.multiple_of(row0 + i * rows, rows), rows)
                old = top[here, :]
                s = lax.dot_general(
                    q_rows[here, :],
                    kv_buf[keys, :],
                    (((1,), (1,)), ((), ())),
                    preferred_element_type=jnp.float32,
                )
                new = jnp.maximum(old, jnp.max(s, axis=1, keepdims=True))
                shift = jnp.concatenate([new * BASE2] * (2 * n), axis=1)
                weights = jnp.exp2(s * BASE2 - shift).astype(jnp.bfloat16)
                factor = jnp.exp2((old - new) * BASE2)
                update = jnp.dot(weights, v_buf[keys, :], preferred_element_type=jnp.float32)
                top[here, :] = new
                state[here, :] = state[here, :] * factor + update
                return carry

            lax.fori_loop(0, tiles, step, 0)

        count = end - start
        eights = count // LOCAL

        def whole(c, carry):
            variant(LOCAL, start + LOCAL * c)
            return carry

        lax.fori_loop(0, eights, whole, 0)
        for n in (4, 2, 1):
            done = (count // (2 * n)) * (2 * n)
            pl.when(count % (2 * n) >= n)(functools.partial(variant, n, start + done))

    def side(i, carry):
        shift = LOCAL * sides[0] * i
        for j in range(len(sides)):
            ends = sum(sides[: j + 1])
            pl.when(i == j)(functools.partial(plane_ready, ends - sides[j], ends))

        def limits(t, w):
            at = (((side0 + 2 * i) * 2 * X + tile0 + t) * 2 + w) * 2
            return bounds[at] + shift, bounds[at + 1] + shift

        def equal(one, other):
            return jnp.logical_and(one[0] == other[0], one[1] == other[1])

        alike = [equal(limits(t, 0), limits(t, 1)) for t in range(X)]
        joined = [
            jnp.logical_and(
                jnp.logical_and(alike[t - 1], alike[t]), equal(limits(t - 1, 0), limits(t, 0))
            ).astype(jnp.int32)
            for t in range(1, X)
        ]
        run3 = 1
        run2 = 1 + joined[2] * run3
        run1 = 1 + joined[1] * run2
        run0 = 1 + joined[0] * run1

        def tile(t, carry):
            run = jnp.where(t == 0, run0, jnp.where(t == 1, run1, jnp.where(t == 2, run2, run3)))
            inside = jnp.where(
                t == 0,
                0,
                jnp.where(t == 1, joined[0], jnp.where(t == 2, joined[1], joined[2])),
            )
            first, second = limits(t, 0), limits(t, 1)
            whole = equal(first, second)
            row0 = pl.multiple_of(t * rows_tile, rows_tile)

            @pl.when(jnp.logical_and(whole, inside == 0))
            def _():
                visit(rows_tile, row0, run, *first)

            @pl.when(jnp.logical_not(whole))
            def _():
                def one(w, carry):
                    visit(
                        TOK_VIEW,
                        row0 + w * TOK_VIEW,
                        1,
                        jnp.where(w == 0, first[0], second[0]),
                        jnp.where(w == 0, first[1], second[1]),
                    )
                    return carry

                lax.fori_loop(0, 2, one, 0)

            return carry

        lax.fori_loop(0, X, tile, 0)
        return carry

    bounds_copy.wait()
    lax.fori_loop(0, len(sides), side, 0)
    for t in range(X):
        lane = lax.broadcasted_iota(jnp.int32, (rows_tile, LANES), 1)
        row = t * rows_tile
        state[row : row + rows_tile, :] = jnp.where(
            lane < HD // 2, top[row : row + rows_tile, :], state[row : row + rows_tile, :]
        )
        state_out(t).start()
    for t in range(X):
        state_out(t).wait()


def attend(bounds, q, q_row, tile0, kv_planes, sides, side0, state, name):
    planes = len(kv_planes)
    anywhere = pl.BlockSpec(memory_space=pl.ANY)
    inputs = [bounds, q, *kv_planes] + ([] if state is None else [state])
    rows = X * 2 * TOK_VIEW
    return pl.pallas_call(
        functools.partial(
            attend_kernel,
            sides=sides,
            side0=side0,
            tile0=tile0,
            q_row=q_row,
            has_state=state is not None,
        ),
        out_shape=jax.ShapeDtypeStruct((rows, LANES), jnp.float32),
        in_specs=[anywhere] * len(inputs),
        out_specs=anywhere,
        scratch_shapes=[
            pltpu.SMEM(bounds.shape, jnp.int32),
            pltpu.SemaphoreType.DMA(()),
            pltpu.VMEM((X, TOK_VIEW, LANES), jnp.bfloat16),
            pltpu.VMEM((rows, LANES), jnp.bfloat16),
            pltpu.VMEM((planes * LOCAL * TOK_VIEW, LANES), jnp.bfloat16),
            pltpu.VMEM((planes * LOCAL * TOK_VIEW, LANES), jnp.bfloat16),
            pltpu.VMEM((rows, LANES), jnp.float32),
            pltpu.VMEM((rows, LANES), jnp.float32),
            pltpu.SemaphoreType.DMA((planes,)),
            pltpu.SemaphoreType.DMA(()),
            pltpu.SemaphoreType.DMA((X,)),
            pltpu.SemaphoreType.DMA((X,)),
        ],
        compiler_params=pltpu.CompilerParams(vmem_limit_bytes=VMEM_BYTES),
        cost_estimate=pl.CostEstimate(
            flops=planes * 2 * rows * (LOCAL * TOK_VIEW) * 2 * TOK_VIEW,
            transcendentals=planes * rows * (LOCAL * TOK_VIEW),
            bytes_accessed=planes << 20,
        ),
        name=name,
    )(*inputs)


def join_kernel(own_hbm, got_hbm, out_ref, own_buf, got_buf, own_sems, got_sems):
    rows_tile = 2 * TOK_VIEW

    def copies(t):
        rows = pl.ds(t * rows_tile, rows_tile)
        return (
            pltpu.make_async_copy(own_hbm.at[rows, :], own_buf.at[rows, :], own_sems.at[t]),
            pltpu.make_async_copy(got_hbm.at[rows, :], got_buf.at[rows, :], got_sems.at[t]),
        )

    for t in range(X):
        for copy in copies(t):
            copy.start()
    low = low_lanes((HD, LANES))
    for t in range(X):
        for copy in copies(t):
            copy.wait()
        rows = slice(t * rows_tile, (t + 1) * rows_tile)
        a, b = own_buf[rows, :], got_buf[rows, :]
        m_a, m_b = a[:, :1], b[:, :1]
        change = (m_b - m_a) * BASE2
        total = a * jnp.exp2(jnp.minimum(-change, 0.0)) + b * jnp.exp2(jnp.minimum(change, 0.0))
        done = total * (1.0 / total[:, HD // 2 : HD // 2 + 1])
        for i in range(4):
            upper = done[i * LANES : i * LANES + HD]
            lower = done[i * LANES + HD : (i + 1) * LANES]
            out_ref[4 * t + i] = jnp.where(low, swap_halves(upper), lower).astype(jnp.bfloat16)


def project_kernel(y_ref, parts_ref, *refs):
    weights, (out_ref, rows_ref, sum_ref) = refs[:4], refs[4:]
    low = low_lanes((HD, LANES))
    for k in range(4):
        y = (y_ref[0] + 4 - k) % 4
        for pair in range(2):
            a = parts_ref[2 * pair * 4 + y].astype(jnp.float32)
            b = parts_ref[(2 * pair + 1) * 4 + y].astype(jnp.float32)
            cols = slice(pair * LANES, (pair + 1) * LANES)
            rows_ref[k, :HD, cols] = jnp.where(low, a, swap_halves(b)).astype(jnp.bfloat16)
            rows_ref[k, HD:, cols] = jnp.where(low, swap_halves(a), b).astype(jnp.bfloat16)
    for k in range(4):
        part = jnp.dot(rows_ref[k], weights[k][...], preferred_element_type=jnp.float32)
        if k == 0:
            sum_ref[...] = part
        elif k < 3:
            sum_ref[...] += part
        else:
            out_ref[...] = (sum_ref[...] + part).astype(jnp.bfloat16)


def key_ranges(view_object, plane, core):
    tile = jnp.arange(2 * X)
    inner = 4 * (tile % X) + 2 * jnp.where(tile < X, core, 1 - core)
    view = PLANE * plane + inner[:, None] + jnp.arange(2)[None, :]
    own = jnp.sum(
        jnp.where(
            jnp.arange(view_object.shape[0])[None, None, :] == view[:, :, None],
            view_object[None, None, :],
            0,
        ),
        axis=-1,
    )
    first = jnp.sum(view_object[None, None, :] < own[:, :, None], axis=-1)
    end = jnp.sum(view_object[None, None, :] <= own[:, :, None], axis=-1)
    edges = jnp.stack([first, end], axis=-1)
    offset = PLANE * (plane + jnp.array([-2, 0, 1]))
    most = PLANE * jnp.array([2, 1, 2])
    edges = jnp.clip(edges[None] - offset[:, None, None, None], 0, most[:, None, None, None])
    local = 2 * (edges // 4) + jnp.clip(edges % 4 - 2 * core, 0, 2)
    return local.astype(jnp.int32).reshape(-1)


def body(queries, keys, values, camera, view_object, out_weight):
    vmem = pl.BlockSpec(memory_space=pltpu.VMEM)
    z_count = lax.axis_size("z")
    up = [(i, (i + 1) % z_count) for i in range(z_count)]
    down = [(i, (i - 1) % z_count) for i in range(z_count)]
    cores = [(0, 1), (1, 0)]
    plane, core = lax.axis_index("z"), lax.axis_index("c")
    sent = pl.pallas_call(
        pack_kernel,
        out_shape=jax.ShapeDtypeStruct((X, 3 * TOK_VIEW, LANES), jnp.bfloat16),
        in_specs=[vmem] * 4,
        out_specs=vmem,
        compiler_params=pltpu.CompilerParams(vmem_limit_bytes=VMEM_BYTES),
        name="pack",
    )(queries, keys, values, camera)
    ours = lax.all_to_all(sent, "x", 0, 0, tiled=True)
    _, view_object = lax.optimization_barrier((sent, view_object))
    bounds = key_ranges(view_object, plane, core)
    kv = ours[:, : 2 * TOK_VIEW].reshape(-1, LANES)
    below = lax.ppermute(kv, "z", up)
    above = lax.ppermute(kv, "z", down)
    q_oth = lax.ppermute(ours[:, 2 * TOK_VIEW :], "c", cores)
    own = attend(bounds, ours, 2 * TOK_VIEW, 0, [kv], (1,), 1, None, "here_own")
    own = attend(bounds, ours, 2 * TOK_VIEW, 0, [kv], (1,), 1, None, "here_own")
    _, sent_weight = lax.optimization_barrier((bounds, out_weight))
    weights = [
        lax.ppermute(sent_weight, "y", [(i, (i + k) % 4) for i in range(4)]) for k in (1, 2, 3)
    ]
    below, above, own = lax.optimization_barrier((below, above, own))
    below_far = lax.ppermute(below, "z", up)
    above_far = lax.ppermute(above, "z", down)
    oth = attend(bounds, q_oth, 0, X, [kv], (1,), 1, None, "here_other")
    oth, sent_weight = lax.optimization_barrier((oth, out_weight))
    weights = [out_weight] + [
        lax.ppermute(sent_weight, "y", [(i, (i + k) % 4) for i in range(4)]) for k in (1, 2, 3)
    ]
    rest = [below_far, below, above, above_far]
    oth = attend(bounds, q_oth, 0, X, rest, (2, 2), 0, oth, "rest_other")
    got = lax.ppermute(oth, "c", cores)
    own = attend(bounds, ours, 2 * TOK_VIEW, 0, rest, (2, 2), 0, own, "rest_own")
    anywhere = pl.BlockSpec(memory_space=pl.ANY)
    attended = pl.pallas_call(
        join_kernel,
        out_shape=jax.ShapeDtypeStruct((16, HD, LANES), jnp.bfloat16),
        in_specs=[anywhere, anywhere],
        out_specs=vmem,
        scratch_shapes=[
            pltpu.VMEM(own.shape, jnp.float32),
            pltpu.VMEM(own.shape, jnp.float32),
            pltpu.SemaphoreType.DMA((X,)),
            pltpu.SemaphoreType.DMA((X,)),
        ],
        compiler_params=pltpu.CompilerParams(vmem_limit_bytes=VMEM_BYTES),
        name="join",
    )(own, got)
    parts = lax.all_to_all(attended, ("x", "y"), 0, 0, tiled=True)
    return pl.pallas_call(
        project_kernel,
        out_shape=jax.ShapeDtypeStruct((LANES, 1024), jnp.bfloat16),
        in_specs=[pl.BlockSpec(memory_space=pltpu.SMEM)] + [vmem] * 5,
        out_specs=vmem,
        scratch_shapes=[
            pltpu.VMEM((4, LANES, 256), jnp.bfloat16),
            pltpu.VMEM((LANES, 1024), jnp.float32),
        ],
        compiler_params=pltpu.CompilerParams(vmem_limit_bytes=VMEM_BYTES),
        name="project",
    )(lax.axis_index("y").astype(jnp.int32).reshape(1), parts, *weights)


def solution(mesh):
    views = mesh.shape["obj"] // (X * C)
    grid = Mesh(mesh.devices.reshape(views, X, C, mesh.shape["head"]), ("z", "x", "c", "y"))
    obj = ("z", "x", "c")
    return jax.shard_map(
        body,
        mesh=grid,
        in_specs=(
            P(obj, "y"),
            P(obj, "y"),
            P(obj, "y"),
            P(obj, "y"),
            P(),
            P("y", None),
        ),
        out_specs=P((*obj, "y"), None),
        check_vma=False,
    )
```

```python
import functools
import math

import jax
import jax.numpy as jnp
from jax import lax
from jax.experimental import pallas as pl
from jax.experimental.pallas import tpu as pltpu
from jax.sharding import Mesh, PartitionSpec as P

HD = 64
TOK_VIEW = 256
X = 4
C = 2
PLANE = 16
LOCAL = 8
LANES = 128
BASE2 = math.log2(math.e) / math.sqrt(HD)
NEG = -1e30
RANGES = ((-2, 2), (0, 1), (1, 2), (-1, 3), (-2, 1), (2, 1))
VMEM_BYTES = 40 << 20


def swap_halves(x):
    return jnp.concatenate([x[:, HD:], x[:, :HD]], axis=1)


def low_lanes(shape):
    return lax.broadcasted_iota(jnp.int32, shape, 1) < HD


def pack_kernel(q_hbm, k_hbm, v_hbm, cam_hbm, out_ref, q_ref, k_ref, v_ref, cam_ref, sems):
    copies = [
        pltpu.make_async_copy(source, target, sems.at[i])
        for i, (source, target) in enumerate(
            [(cam_hbm, cam_ref), (k_hbm, k_ref), (v_hbm, v_ref), (q_hbm, q_ref)]
        )
    ]
    for copy in copies:
        copy.start()
    for copy in copies:
        copy.wait()
    cam = cam_ref[...].astype(jnp.float32)
    low = low_lanes((TOK_VIEW, LANES))
    for pair in range(2):
        cols = slice(pair * LANES, (pair + 1) * LANES)
        queries = []
        for view in range(2):
            rows = slice(view * TOK_VIEW, (view + 1) * TOK_VIEW)
            shift = cam[view : view + 1, cols]
            k = k_ref[rows, cols].astype(jnp.float32) + shift
            v = v_ref[rows, cols].astype(jnp.float32)
            out_ref[2 * pair, rows, :] = jnp.where(low, k, swap_halves(v)).astype(jnp.bfloat16)
            out_ref[2 * pair + 1, rows, :] = jnp.where(low, swap_halves(k), v).astype(jnp.bfloat16)
            queries.append(q_ref[rows, cols].astype(jnp.float32) + shift)
        first, second = queries
        rows = slice(2 * TOK_VIEW, 3 * TOK_VIEW)
        out_ref[2 * pair, rows, :] = jnp.where(low, first, swap_halves(second)).astype(jnp.bfloat16)
        out_ref[2 * pair + 1, rows, :] = jnp.where(low, swap_halves(first), second).astype(
            jnp.bfloat16
        )


def attend_kernel(bounds_hbm, q_hbm, *refs, sides, side0, side_step, tile0, q_row, has_state):
    planes = sum(sides)
    kv_hbm = refs[:planes]
    refs = refs[planes:]
    if has_state:
        state_hbm, refs = refs[0], refs[1:]
    out_hbm, bounds, bounds_sem, q_buf, q_rows, kv_buf, v_buf, state, top, kv_sems, q_sem, in_sems, out_sems = refs
    size, rows_tile = LOCAL * TOK_VIEW, 2 * TOK_VIEW
    kv_copies = [
        pltpu.make_async_copy(kv_hbm[p], kv_buf.at[pl.ds(p * size, size), :], kv_sems.at[p])
        for p in range(planes)
    ]
    q_copy = pltpu.make_async_copy(q_hbm.at[:, pl.ds(q_row, TOK_VIEW), :], q_buf, q_sem)

    def rows_of(t):
        return pl.ds(pl.multiple_of(t * rows_tile, rows_tile), rows_tile)

    def state_in(t):
        return pltpu.make_async_copy(
            state_hbm.at[rows_of(t), :], state.at[rows_of(t), :], in_sems.at[t]
        )

    def state_out(t):
        return pltpu.make_async_copy(
            state.at[rows_of(t), :], out_hbm.at[rows_of(t), :], out_sems.at[t]
        )

    bounds_copy = pltpu.make_async_copy(bounds_hbm, bounds, bounds_sem)
    bounds_copy.start()
    q_copy.start()
    if has_state:
        for t in range(X):
            state_in(t).start()
    for copy in kv_copies:
        copy.start()
    lane = lax.broadcasted_iota(jnp.int32, (1, LANES), 1)
    keep = jnp.where(lane < HD, 0.0, 1.0).astype(jnp.bfloat16)
    ones = jnp.where(lane < HD, 1.0, 0.0).astype(jnp.bfloat16)

    def plane_ready(first, end):
        for p in range(first, end):
            kv_copies[p].wait()

        def fill(i, carry):
            part = pl.ds(pl.multiple_of(i * 2 * TOK_VIEW, 2 * TOK_VIEW), 2 * TOK_VIEW)
            v_buf[part, :] = kv_buf[part, :] * keep + ones
            return carry

        lax.fori_loop(first * LOCAL // 2, end * LOCAL // 2, fill, 0)

    q_copy.wait()
    for t in range(X):
        packed = q_buf[t]
        low = low_lanes((TOK_VIEW, LANES))
        zero = jnp.zeros((), jnp.bfloat16)
        row = t * rows_tile
        q_rows[row : row + TOK_VIEW, :] = jnp.where(low, packed, zero)
        q_rows[row + TOK_VIEW : row + rows_tile, :] = jnp.where(low, swap_halves(packed), zero)
        if has_state:
            state_in(t).wait()
            packed = state[row : row + rows_tile, :]
            top[row : row + rows_tile, :] = jnp.broadcast_to(packed[:, :1], packed.shape)
        else:
            top[row : row + rows_tile, :] = jnp.full((rows_tile, LANES), NEG, jnp.float32)
            state[row : row + rows_tile, :] = jnp.zeros((rows_tile, LANES), jnp.float32)

    def visit(rows, row0, tiles, start, end):
        def variant(n, key0):
            keys = pl.ds(pl.multiple_of(key0 * TOK_VIEW, TOK_VIEW), n * TOK_VIEW)

            def step(i, carry):
                here = pl.ds(pl.multiple_of(row0 + i * rows, rows), rows)
                old = top[here, :]
                s = lax.dot_general(
                    q_rows[here, :],
                    kv_buf[keys, :],
                    (((1,), (1,)), ((), ())),
                    preferred_element_type=jnp.float32,
                )
                new = jnp.maximum(old, jnp.max(s, axis=1, keepdims=True))
                shift = jnp.concatenate([new * BASE2] * (2 * n), axis=1)
                weights = jnp.exp2(s * BASE2 - shift).astype(jnp.bfloat16)
                factor = jnp.exp2((old - new) * BASE2)
                update = jnp.dot(weights, v_buf[keys, :], preferred_element_type=jnp.float32)
                top[here, :] = new
                state[here, :] = state[here, :] * factor + update
                return carry

            lax.fori_loop(0, tiles, step, 0)

        count = end - start
        eights = count // LOCAL

        def whole(c, carry):
            variant(LOCAL, start + LOCAL * c)
            return carry

        lax.fori_loop(0, eights, whole, 0)
        for n in (4, 2, 1):
            done = (count // (2 * n)) * (2 * n)
            pl.when(count % (2 * n) >= n)(functools.partial(variant, n, start + done))

    def side(i, carry):
        shift = LOCAL * sides[0] * i
        for j in range(len(sides)):
            ends = sum(sides[: j + 1])
            pl.when(i == j)(functools.partial(plane_ready, ends - sides[j], ends))

        def limits(t, w):
            at = (((side0 + side_step * i) * 2 * X + tile0 + t) * 2 + w) * 2
            return bounds[at] + shift, bounds[at + 1] + shift

        def equal(one, other):
            return jnp.logical_and(one[0] == other[0], one[1] == other[1])

        alike = [equal(limits(t, 0), limits(t, 1)) for t in range(X)]
        joined = [
            jnp.logical_and(
                jnp.logical_and(alike[t - 1], alike[t]), equal(limits(t - 1, 0), limits(t, 0))
            ).astype(jnp.int32)
            for t in range(1, X)
        ]
        run3 = 1
        run2 = 1 + joined[2] * run3
        run1 = 1 + joined[1] * run2
        run0 = 1 + joined[0] * run1

        def tile(t, carry):
            run = jnp.where(t == 0, run0, jnp.where(t == 1, run1, jnp.where(t == 2, run2, run3)))
            inside = jnp.where(
                t == 0,
                0,
                jnp.where(t == 1, joined[0], jnp.where(t == 2, joined[1], joined[2])),
            )
            first, second = limits(t, 0), limits(t, 1)
            whole = equal(first, second)
            row0 = pl.multiple_of(t * rows_tile, rows_tile)

            @pl.when(jnp.logical_and(whole, inside == 0))
            def _():
                visit(rows_tile, row0, run, *first)

            @pl.when(jnp.logical_not(whole))
            def _():
                def one(w, carry):
                    visit(
                        TOK_VIEW,
                        row0 + w * TOK_VIEW,
                        1,
                        jnp.where(w == 0, first[0], second[0]),
                        jnp.where(w == 0, first[1], second[1]),
                    )
                    return carry

                lax.fori_loop(0, 2, one, 0)

            return carry

        lax.fori_loop(0, X, tile, 0)
        return carry

    bounds_copy.wait()
    lax.fori_loop(0, len(sides), side, 0)
    for t in range(X):
        lane = lax.broadcasted_iota(jnp.int32, (rows_tile, LANES), 1)
        row = t * rows_tile
        state[row : row + rows_tile, :] = jnp.where(
            lane < HD // 2, top[row : row + rows_tile, :], state[row : row + rows_tile, :]
        )
        state_out(t).start()
    for t in range(X):
        state_out(t).wait()


def attend(bounds, q, q_row, tile0, kv_planes, sides, side0, side_step, state, name):
    planes = len(kv_planes)
    anywhere = pl.BlockSpec(memory_space=pl.ANY)
    inputs = [bounds, q, *kv_planes] + ([] if state is None else [state])
    rows = X * 2 * TOK_VIEW
    return pl.pallas_call(
        functools.partial(
            attend_kernel,
            sides=sides,
            side0=side0,
            side_step=side_step,
            tile0=tile0,
            q_row=q_row,
            has_state=state is not None,
        ),
        out_shape=jax.ShapeDtypeStruct((rows, LANES), jnp.float32),
        in_specs=[anywhere] * len(inputs),
        out_specs=anywhere,
        scratch_shapes=[
            pltpu.SMEM(bounds.shape, jnp.int32),
            pltpu.SemaphoreType.DMA(()),
            pltpu.VMEM((X, TOK_VIEW, LANES), jnp.bfloat16),
            pltpu.VMEM((rows, LANES), jnp.bfloat16),
            pltpu.VMEM((planes * LOCAL * TOK_VIEW, LANES), jnp.bfloat16),
            pltpu.VMEM((planes * LOCAL * TOK_VIEW, LANES), jnp.bfloat16),
            pltpu.VMEM((rows, LANES), jnp.float32),
            pltpu.VMEM((rows, LANES), jnp.float32),
            pltpu.SemaphoreType.DMA((planes,)),
            pltpu.SemaphoreType.DMA(()),
            pltpu.SemaphoreType.DMA((X,)),
            pltpu.SemaphoreType.DMA((X,)),
        ],
        compiler_params=pltpu.CompilerParams(vmem_limit_bytes=VMEM_BYTES),
        cost_estimate=pl.CostEstimate(
            flops=planes * 2 * rows * (LOCAL * TOK_VIEW) * 2 * TOK_VIEW,
            transcendentals=planes * rows * (LOCAL * TOK_VIEW),
            bytes_accessed=planes << 20,
        ),
        name=name,
    )(*inputs)


def join_kernel(own_hbm, got_hbm, out_ref, own_buf, got_buf, own_sems, got_sems):
    rows_tile = 2 * TOK_VIEW

    def copies(t):
        rows = pl.ds(t * rows_tile, rows_tile)
        return (
            pltpu.make_async_copy(own_hbm.at[rows, :], own_buf.at[rows, :], own_sems.at[t]),
            pltpu.make_async_copy(got_hbm.at[rows, :], got_buf.at[rows, :], got_sems.at[t]),
        )

    for t in range(X):
        for copy in copies(t):
            copy.start()
    low = low_lanes((HD, LANES))
    for t in range(X):
        for copy in copies(t):
            copy.wait()
        rows = slice(t * rows_tile, (t + 1) * rows_tile)
        a, b = own_buf[rows, :], got_buf[rows, :]
        m_a, m_b = a[:, :1], b[:, :1]
        change = (m_b - m_a) * BASE2
        total = a * jnp.exp2(jnp.minimum(-change, 0.0)) + b * jnp.exp2(jnp.minimum(change, 0.0))
        done = total * (1.0 / total[:, HD // 2 : HD // 2 + 1])
        for i in range(4):
            upper = done[i * LANES : i * LANES + HD]
            lower = done[i * LANES + HD : (i + 1) * LANES]
            out_ref[4 * t + i] = jnp.where(low, swap_halves(upper), lower).astype(jnp.bfloat16)


def project_kernel(y_ref, parts_ref, *refs):
    weights, (out_ref, rows_ref, sum_ref) = refs[:4], refs[4:]
    low = low_lanes((HD, LANES))
    for k in range(4):
        y = (y_ref[0] + 4 - k) % 4
        for pair in range(2):
            a = parts_ref[2 * pair * 4 + y].astype(jnp.float32)
            b = parts_ref[(2 * pair + 1) * 4 + y].astype(jnp.float32)
            cols = slice(pair * LANES, (pair + 1) * LANES)
            rows_ref[k, :HD, cols] = jnp.where(low, a, swap_halves(b)).astype(jnp.bfloat16)
            rows_ref[k, HD:, cols] = jnp.where(low, swap_halves(a), b).astype(jnp.bfloat16)
    for k in range(4):
        part = jnp.dot(rows_ref[k], weights[k][...], preferred_element_type=jnp.float32)
        if k == 0:
            sum_ref[...] = part
        elif k < 3:
            sum_ref[...] += part
        else:
            out_ref[...] = (sum_ref[...] + part).astype(jnp.bfloat16)


def key_ranges(view_object, plane, core):
    tile = jnp.arange(2 * X)
    inner = 4 * (tile % X) + 2 * jnp.where(tile < X, core, 1 - core)
    view = PLANE * plane + inner[:, None] + jnp.arange(2)[None, :]
    own = jnp.sum(
        jnp.where(
            jnp.arange(view_object.shape[0])[None, None, :] == view[:, :, None],
            view_object[None, None, :],
            0,
        ),
        axis=-1,
    )
    first = jnp.sum(view_object[None, None, :] < own[:, :, None], axis=-1)
    end = jnp.sum(view_object[None, None, :] <= own[:, :, None], axis=-1)
    edges = jnp.stack([first, end], axis=-1)
    offset = PLANE * (plane + jnp.array([first for first, _ in RANGES]))
    most = PLANE * jnp.array([count for _, count in RANGES])
    edges = jnp.clip(edges[None] - offset[:, None, None, None], 0, most[:, None, None, None])
    local = 2 * (edges // 4) + jnp.clip(edges % 4 - 2 * core, 0, 2)
    return local.astype(jnp.int32).reshape(-1)


def body(queries, keys, values, camera, view_object, out_weight):
    vmem = pl.BlockSpec(memory_space=pltpu.VMEM)
    z_count = lax.axis_size("z")
    up = [(i, (i + 1) % z_count) for i in range(z_count)]
    down = [(i, (i - 1) % z_count) for i in range(z_count)]
    cores = [(0, 1), (1, 0)]
    plane, core = lax.axis_index("z"), lax.axis_index("c")
    sent = pl.pallas_call(
        pack_kernel,
        out_shape=jax.ShapeDtypeStruct((X, 3 * TOK_VIEW, LANES), jnp.bfloat16),
        in_specs=[pl.BlockSpec(memory_space=pl.ANY)] * 4,
        out_specs=vmem,
        scratch_shapes=[
            *(pltpu.VMEM(x.shape, jnp.bfloat16) for x in (queries, keys, values, camera)),
            pltpu.SemaphoreType.DMA((4,)),
        ],
        compiler_params=pltpu.CompilerParams(vmem_limit_bytes=60 << 20),
        name="pack",
    )(queries, keys, values, camera)
    ours = lax.all_to_all(sent, "x", 0, 0, tiled=True)
    _, view_object = lax.optimization_barrier((sent, view_object))
    bounds = key_ranges(view_object, plane, core)
    kv = ours[:, : 2 * TOK_VIEW].reshape(-1, LANES)
    below = lax.ppermute(kv, "z", up)
    above = lax.ppermute(kv, "z", down)
    q_oth = lax.ppermute(ours[:, 2 * TOK_VIEW :], "c", cores)
    own_row = 2 * TOK_VIEW
    own = attend(bounds, ours, own_row, 0, [kv], (1,), 1, 0, None, "here_own")
    own, sent_weight = lax.optimization_barrier((own, out_weight))
    weights = [out_weight] + [
        lax.ppermute(sent_weight, "y", [(i, (i + k) % 4) for i in range(4)]) for k in (1, 2, 3)
    ]
    below, above, own = lax.optimization_barrier((below, above, own))
    below_far = lax.ppermute(below, "z", up)
    above_far = lax.ppermute(above, "z", down)
    oth = attend(bounds, q_oth, 0, X, [below, kv, above], (3,), 3, 0, None, "near_other")
    oth = attend(bounds, q_oth, 0, X, [below_far, above_far], (1, 1), 4, 1, oth, "far_other")
    got = lax.ppermute(oth, "c", cores)
    rest = [below_far, below, above, above_far]
    own = attend(bounds, ours, own_row, 0, rest, (2, 2), 0, 2, own, "rest_own")
    anywhere = pl.BlockSpec(memory_space=pl.ANY)
    attended = pl.pallas_call(
        join_kernel,
        out_shape=jax.ShapeDtypeStruct((16, HD, LANES), jnp.bfloat16),
        in_specs=[anywhere, anywhere],
        out_specs=vmem,
        scratch_shapes=[
            pltpu.VMEM(own.shape, jnp.float32),
            pltpu.VMEM(own.shape, jnp.float32),
            pltpu.SemaphoreType.DMA((X,)),
            pltpu.SemaphoreType.DMA((X,)),
        ],
        compiler_params=pltpu.CompilerParams(vmem_limit_bytes=VMEM_BYTES),
        name="join",
    )(own, got)
    parts = lax.all_to_all(attended, ("x", "y"), 0, 0, tiled=True)
    return pl.pallas_call(
        project_kernel,
        out_shape=jax.ShapeDtypeStruct((LANES, 1024), jnp.bfloat16),
        in_specs=[pl.BlockSpec(memory_space=pltpu.SMEM)] + [vmem] * 5,
        out_specs=vmem,
        scratch_shapes=[
            pltpu.VMEM((4, LANES, 256), jnp.bfloat16),
            pltpu.VMEM((LANES, 1024), jnp.float32),
        ],
        compiler_params=pltpu.CompilerParams(vmem_limit_bytes=VMEM_BYTES),
        name="project",
    )(lax.axis_index("y").astype(jnp.int32).reshape(1), parts, *weights)


def solution(mesh):
    views = mesh.shape["obj"] // (X * C)
    grid = Mesh(mesh.devices.reshape(views, X, C, mesh.shape["head"]), ("z", "x", "c", "y"))
    obj = ("z", "x", "c")
    return jax.shard_map(
        body,
        mesh=grid,
        in_specs=(
            P(obj, "y"),
            P(obj, "y"),
            P(obj, "y"),
            P(obj, "y"),
            P(),
            P("y", None),
        ),
        out_specs=P((*obj, "y"), None),
        check_vma=False,
    )
```

```python
import functools
import math

import jax
import jax.numpy as jnp
from jax import lax
from jax.experimental import pallas as pl
from jax.experimental.pallas import tpu as pltpu
from jax.sharding import Mesh, PartitionSpec as P

HD = 64
TOK_VIEW = 256
X = 4
C = 2
PLANE = 16
LOCAL = 8
LANES = 128
BASE2 = math.log2(math.e) / math.sqrt(HD)
NEG = -1e30
RANGES = ((-2, 2), (0, 1), (1, 2), (-1, 3), (-2, 1), (2, 1))
VMEM_BYTES = 40 << 20


def swap_halves(x):
    return jnp.concatenate([x[:, HD:], x[:, :HD]], axis=1)


def low_lanes(shape):
    return lax.broadcasted_iota(jnp.int32, shape, 1) < HD


def pack_kernel(q_hbm, k_hbm, v_hbm, cam_hbm, out_ref, q_ref, k_ref, v_ref, cam_ref, sems):
    copies = [
        pltpu.make_async_copy(source, target, sems.at[i])
        for i, (source, target) in enumerate(
            [(cam_hbm, cam_ref), (k_hbm, k_ref), (v_hbm, v_ref), (q_hbm, q_ref)]
        )
    ]
    for copy in copies:
        copy.start()
    for copy in copies:
        copy.wait()
    cam = cam_ref[...].astype(jnp.float32)
    low = low_lanes((TOK_VIEW, LANES))
    for pair in range(2):
        cols = slice(pair * LANES, (pair + 1) * LANES)
        queries = []
        for view in range(2):
            rows = slice(view * TOK_VIEW, (view + 1) * TOK_VIEW)
            shift = cam[view : view + 1, cols]
            k = k_ref[rows, cols].astype(jnp.float32) + shift
            v = v_ref[rows, cols].astype(jnp.float32)
            out_ref[2 * pair, rows, :] = jnp.where(low, k, swap_halves(v)).astype(jnp.bfloat16)
            out_ref[2 * pair + 1, rows, :] = jnp.where(low, swap_halves(k), v).astype(jnp.bfloat16)
            queries.append(q_ref[rows, cols].astype(jnp.float32) + shift)
        first, second = queries
        rows = slice(2 * TOK_VIEW, 3 * TOK_VIEW)
        out_ref[2 * pair, rows, :] = jnp.where(low, first, swap_halves(second)).astype(jnp.bfloat16)
        out_ref[2 * pair + 1, rows, :] = jnp.where(low, swap_halves(first), second).astype(
            jnp.bfloat16
        )


def attend_kernel(bounds_hbm, q_ref, *refs, sides, side0, side_step, tile0, q_row, eight, has_state):
    planes = sum(sides)
    kv_hbm = refs[:planes]
    refs = refs[planes:]
    if has_state:
        before, refs = refs[0], refs[1:]
    state, bounds, bounds_sem, q_rows, kv_buf, v_buf, top, kv_sems = refs
    size, rows_tile = LOCAL * TOK_VIEW, 2 * TOK_VIEW
    kv_copies = [
        pltpu.make_async_copy(kv_hbm[p], kv_buf.at[pl.ds(p * size, size), :], kv_sems.at[p])
        for p in range(planes)
    ]
    bounds_copy = pltpu.make_async_copy(bounds_hbm, bounds, bounds_sem)
    bounds_copy.start()
    for copy in kv_copies:
        copy.start()
    lane = lax.broadcasted_iota(jnp.int32, (1, LANES), 1)
    keep = jnp.where(lane < HD, 0.0, 1.0).astype(jnp.bfloat16)
    ones = jnp.where(lane < HD, 1.0, 0.0).astype(jnp.bfloat16)

    def plane_ready(first, end):
        for p in range(first, end):
            kv_copies[p].wait()

        def fill(i, carry):
            part = pl.ds(pl.multiple_of(i * 2 * TOK_VIEW, 2 * TOK_VIEW), 2 * TOK_VIEW)
            v_buf[part, :] = kv_buf[part, :] * keep + ones
            return carry

        lax.fori_loop(first * LOCAL // 2, end * LOCAL // 2, fill, 0)

    for t in range(X):
        packed = q_ref[t, q_row : q_row + TOK_VIEW, :]
        low = low_lanes((TOK_VIEW, LANES))
        zero = jnp.zeros((), jnp.bfloat16)
        row = t * rows_tile
        q_rows[row : row + TOK_VIEW, :] = jnp.where(low, packed, zero)
        q_rows[row + TOK_VIEW : row + rows_tile, :] = jnp.where(low, swap_halves(packed), zero)
        if has_state:
            packed = before[row : row + rows_tile, :]
            state[row : row + rows_tile, :] = packed
            top[row : row + rows_tile, :] = jnp.broadcast_to(packed[:, :1], packed.shape)
        else:
            top[row : row + rows_tile, :] = jnp.full((rows_tile, LANES), NEG, jnp.float32)
            state[row : row + rows_tile, :] = jnp.zeros((rows_tile, LANES), jnp.float32)

    def visit(rows, row0, tiles, start, end):
        def variant(n, key0, row0, tiles, parts):
            keys = pl.ds(pl.multiple_of(key0 * TOK_VIEW, TOK_VIEW), n * TOK_VIEW)

            def step(i, carry):
                def here(part):
                    at = row0 + (i * parts + part) * rows
                    return pl.ds(pl.multiple_of(at, rows), rows)

                def scores(part):
                    return lax.dot_general(
                        q_rows[here(part), :],
                        kv_buf[keys, :],
                        (((1,), (1,)), ((), ())),
                        preferred_element_type=jnp.float32,
                    )

                ahead = scores(0)
                for part in range(parts):
                    s = ahead
                    if part + 1 < parts:
                        ahead = scores(part + 1)
                    piece = here(part)
                    old = top[piece, :]
                    new = jnp.maximum(old, jnp.max(s, axis=1, keepdims=True))
                    shift = jnp.concatenate([new * BASE2] * (2 * n), axis=1)
                    weights = jnp.exp2(s * BASE2 - shift).astype(jnp.bfloat16)
                    factor = jnp.exp2((old - new) * BASE2)
                    update = jnp.dot(weights, v_buf[keys, :], preferred_element_type=jnp.float32)
                    top[piece, :] = new
                    state[piece, :] = state[piece, :] * factor + update
                return carry

            lax.fori_loop(0, tiles, step, 0)

        count = end - start

        def repeat(times, n, row0, tiles, parts):
            def one(c, carry):
                variant(n, start + n * c, row0, tiles, parts)
                return carry

            lax.fori_loop(0, times, one, 0)

        if rows == rows_tile:
            pairs, odd = tiles // 2, tiles % 2
            eights = 0
            if eight:
                eights = count // 8 * 2
                repeat(jnp.where(pairs > 0, count // 8, 0), 8, row0, pairs, 2)

            def four(c, carry):
                variant(4, start + 4 * c, row0, pairs, 2)
                return carry

            lax.fori_loop(eights, jnp.where(pairs > 0, count // 4, eights), four, 0)
            repeat(odd * (count // 4), 4, row0 + pairs * 2 * rows, 1, 1)
        else:
            repeat(count // 8, 8, row0, tiles, 1)
            pl.when(count % 8 >= 4)(lambda: variant(4, start + count // 8 * 8, row0, tiles, 1))
        for n in (2, 1):
            done = (count // (2 * n)) * (2 * n)
            pl.when(count % (2 * n) >= n)(
                functools.partial(variant, n, start + done, row0, tiles, 1)
            )

    def side(i, carry):
        shift = LOCAL * sides[0] * i
        for j in range(len(sides)):
            ends = sum(sides[: j + 1])
            pl.when(i == j)(functools.partial(plane_ready, ends - sides[j], ends))

        def limits(t, w):
            at = (((side0 + side_step * i) * 2 * X + tile0 + t) * 2 + w) * 2
            return bounds[at] + shift, bounds[at + 1] + shift

        def equal(one, other):
            return jnp.logical_and(one[0] == other[0], one[1] == other[1])

        alike = [equal(limits(t, 0), limits(t, 1)) for t in range(X)]
        joined = [
            jnp.logical_and(
                jnp.logical_and(alike[t - 1], alike[t]), equal(limits(t - 1, 0), limits(t, 0))
            ).astype(jnp.int32)
            for t in range(1, X)
        ]
        run3 = 1
        run2 = 1 + joined[2] * run3
        run1 = 1 + joined[1] * run2
        run0 = 1 + joined[0] * run1

        def tile(t, carry):
            run = jnp.where(t == 0, run0, jnp.where(t == 1, run1, jnp.where(t == 2, run2, run3)))
            inside = jnp.where(
                t == 0,
                0,
                jnp.where(t == 1, joined[0], jnp.where(t == 2, joined[1], joined[2])),
            )
            first, second = limits(t, 0), limits(t, 1)
            whole = equal(first, second)
            row0 = pl.multiple_of(t * rows_tile, rows_tile)

            @pl.when(jnp.logical_and(whole, inside == 0))
            def _():
                visit(rows_tile, row0, run, *first)

            @pl.when(jnp.logical_not(whole))
            def _():
                def one(w, carry):
                    visit(
                        TOK_VIEW,
                        row0 + w * TOK_VIEW,
                        1,
                        jnp.where(w == 0, first[0], second[0]),
                        jnp.where(w == 0, first[1], second[1]),
                    )
                    return carry

                lax.fori_loop(0, 2, one, 0)

            return carry

        lax.fori_loop(0, X, tile, 0)
        return carry

    bounds_copy.wait()
    lax.fori_loop(0, len(sides), side, 0)
    for t in range(X):
        lane = lax.broadcasted_iota(jnp.int32, (rows_tile, LANES), 1)
        row = t * rows_tile
        state[row : row + rows_tile, :] = jnp.where(
            lane < HD // 2, top[row : row + rows_tile, :], state[row : row + rows_tile, :]
        )


def attend(bounds, q, q_row, tile0, kv_planes, sides, side0, side_step, state, eight, name):
    planes = len(kv_planes)
    anywhere = pl.BlockSpec(memory_space=pl.ANY)
    vmem = pl.BlockSpec(memory_space=pltpu.VMEM)
    inputs = [bounds, q, *kv_planes] + ([] if state is None else [state])
    rows = X * 2 * TOK_VIEW
    return pl.pallas_call(
        functools.partial(
            attend_kernel,
            sides=sides,
            side0=side0,
            side_step=side_step,
            tile0=tile0,
            q_row=q_row,
            eight=eight,
            has_state=state is not None,
        ),
        out_shape=jax.ShapeDtypeStruct((rows, LANES), jnp.float32),
        in_specs=[anywhere, vmem, *[anywhere] * planes, *[vmem] * (state is not None)],
        out_specs=vmem,
        scratch_shapes=[
            pltpu.SMEM(bounds.shape, jnp.int32),
            pltpu.SemaphoreType.DMA(()),
            pltpu.VMEM((rows, LANES), jnp.bfloat16),
            pltpu.VMEM((planes * LOCAL * TOK_VIEW, LANES), jnp.bfloat16),
            pltpu.VMEM((planes * LOCAL * TOK_VIEW, LANES), jnp.bfloat16),
            pltpu.VMEM((rows, LANES), jnp.float32),
            pltpu.SemaphoreType.DMA((planes,)),
        ],
        compiler_params=pltpu.CompilerParams(vmem_limit_bytes=VMEM_BYTES),
        cost_estimate=pl.CostEstimate(
            flops=planes * 2 * rows * (LOCAL * TOK_VIEW) * 2 * TOK_VIEW,
            transcendentals=planes * rows * (LOCAL * TOK_VIEW),
            bytes_accessed=planes << 20,
        ),
        name=name,
    )(*inputs)


def join_kernel(own_ref, got_ref, out_ref):
    rows_tile = 2 * TOK_VIEW
    low = low_lanes((HD, LANES))
    for t in range(X):
        rows = slice(t * rows_tile, (t + 1) * rows_tile)
        a, b = own_ref[rows, :], got_ref[rows, :]
        m_a, m_b = a[:, :1], b[:, :1]
        change = (m_b - m_a) * BASE2
        total = a * jnp.exp2(jnp.minimum(-change, 0.0)) + b * jnp.exp2(jnp.minimum(change, 0.0))
        done = total * (1.0 / total[:, HD // 2 : HD // 2 + 1])
        for i in range(4):
            upper = done[i * LANES : i * LANES + HD]
            lower = done[i * LANES + HD : (i + 1) * LANES]
            out_ref[4 * t + i] = jnp.where(low, swap_halves(upper), lower).astype(jnp.bfloat16)


def project_kernel(y_ref, parts_ref, *refs):
    weights, (out_ref, rows_ref, sum_ref) = refs[:4], refs[4:]
    low = low_lanes((HD, LANES))
    for k in range(4):
        y = (y_ref[0] + 4 - k) % 4
        for pair in range(2):
            a = parts_ref[2 * pair * 4 + y].astype(jnp.float32)
            b = parts_ref[(2 * pair + 1) * 4 + y].astype(jnp.float32)
            cols = slice(pair * LANES, (pair + 1) * LANES)
            rows_ref[k, :HD, cols] = jnp.where(low, a, swap_halves(b)).astype(jnp.bfloat16)
            rows_ref[k, HD:, cols] = jnp.where(low, swap_halves(a), b).astype(jnp.bfloat16)
    for k in range(4):
        part = jnp.dot(rows_ref[k], weights[k][...], preferred_element_type=jnp.float32)
        if k == 0:
            sum_ref[...] = part
        elif k < 3:
            sum_ref[...] += part
        else:
            out_ref[...] = (sum_ref[...] + part).astype(jnp.bfloat16)


def key_ranges(view_object, plane, core):
    tile = jnp.arange(2 * X)
    inner = 4 * (tile % X) + 2 * jnp.where(tile < X, core, 1 - core)
    view = PLANE * plane + inner[:, None] + jnp.arange(2)[None, :]
    own = jnp.sum(
        jnp.where(
            jnp.arange(view_object.shape[0])[None, None, :] == view[:, :, None],
            view_object[None, None, :],
            0,
        ),
        axis=-1,
    )
    first = jnp.sum(view_object[None, None, :] < own[:, :, None], axis=-1)
    end = jnp.sum(view_object[None, None, :] <= own[:, :, None], axis=-1)
    edges = jnp.stack([first, end], axis=-1)
    offset = PLANE * (plane + jnp.array([first for first, _ in RANGES]))
    most = PLANE * jnp.array([count for _, count in RANGES])
    edges = jnp.clip(edges[None] - offset[:, None, None, None], 0, most[:, None, None, None])
    local = 2 * (edges // 4) + jnp.clip(edges % 4 - 2 * core, 0, 2)
    return local.astype(jnp.int32).reshape(-1)


def body(queries, keys, values, camera, view_object, out_weight):
    vmem = pl.BlockSpec(memory_space=pltpu.VMEM)
    z_count = lax.axis_size("z")
    up = [(i, (i + 1) % z_count) for i in range(z_count)]
    down = [(i, (i - 1) % z_count) for i in range(z_count)]
    cores = [(0, 1), (1, 0)]
    plane, core = lax.axis_index("z"), lax.axis_index("c")
    sent = pl.pallas_call(
        pack_kernel,
        out_shape=jax.ShapeDtypeStruct((X, 3 * TOK_VIEW, LANES), jnp.bfloat16),
        in_specs=[pl.BlockSpec(memory_space=pl.ANY)] * 4,
        out_specs=vmem,
        scratch_shapes=[
            *(pltpu.VMEM(x.shape, jnp.bfloat16) for x in (queries, keys, values, camera)),
            pltpu.SemaphoreType.DMA((4,)),
        ],
        compiler_params=pltpu.CompilerParams(vmem_limit_bytes=60 << 20),
        name="pack",
    )(queries, keys, values, camera)
    ours = lax.all_to_all(sent, "x", 0, 0, tiled=True)
    _, view_object = lax.optimization_barrier((sent, view_object))
    bounds = key_ranges(view_object, plane, core)
    kv = ours[:, : 2 * TOK_VIEW].reshape(-1, LANES)
    below = lax.ppermute(kv, "z", up)
    above = lax.ppermute(kv, "z", down)
    q_oth = lax.ppermute(ours[:, 2 * TOK_VIEW :], "c", cores)
    own_row = 2 * TOK_VIEW
    own = attend(bounds, ours, own_row, 0, [kv], (1,), 1, 0, None, False, "here_own")
    own, sent_weight = lax.optimization_barrier((own, out_weight))
    weights = [out_weight] + [
        lax.ppermute(sent_weight, "y", [(i, (i + k) % 4) for i in range(4)]) for k in (1, 2, 3)
    ]
    below, above, own = lax.optimization_barrier((below, above, own))
    below_far = lax.ppermute(below, "z", up)
    above_far = lax.ppermute(above, "z", down)
    oth = attend(bounds, q_oth, 0, X, [below, kv, above], (3,), 3, 0, None, False, "near_other")
    oth = attend(bounds, q_oth, 0, X, [below_far, above_far], (1, 1), 4, 1, oth, False, "far_other")
    got = lax.ppermute(oth, "c", cores)
    rest = [below_far, below, above, above_far]
    own = attend(bounds, ours, own_row, 0, rest, (2, 2), 0, 2, own, False, "rest_own")
    attended = pl.pallas_call(
        join_kernel,
        out_shape=jax.ShapeDtypeStruct((16, HD, LANES), jnp.bfloat16),
        in_specs=[vmem, vmem],
        out_specs=vmem,
        compiler_params=pltpu.CompilerParams(vmem_limit_bytes=VMEM_BYTES),
        name="join",
    )(own, got)
    parts = lax.all_to_all(attended, ("x", "y"), 0, 0, tiled=True)
    return pl.pallas_call(
        project_kernel,
        out_shape=jax.ShapeDtypeStruct((LANES, 1024), jnp.bfloat16),
        in_specs=[pl.BlockSpec(memory_space=pltpu.SMEM)] + [vmem] * 5,
        out_specs=vmem,
        scratch_shapes=[
            pltpu.VMEM((4, LANES, 256), jnp.bfloat16),
            pltpu.VMEM((LANES, 1024), jnp.float32),
        ],
        compiler_params=pltpu.CompilerParams(vmem_limit_bytes=VMEM_BYTES),
        name="project",
    )(lax.axis_index("y").astype(jnp.int32).reshape(1), parts, *weights)


def solution(mesh):
    views = mesh.shape["obj"] // (X * C)
    grid = Mesh(mesh.devices.reshape(views, X, C, mesh.shape["head"]), ("z", "x", "c", "y"))
    obj = ("z", "x", "c")
    return jax.shard_map(
        body,
        mesh=grid,
        in_specs=(
            P(obj, "y"),
            P(obj, "y"),
            P(obj, "y"),
            P(obj, "y"),
            P(),
            P("y", None),
        ),
        out_specs=P((*obj, "y"), None),
        check_vma=False,
    )
```

```python
import functools
import math

import jax
import jax.numpy as jnp
from jax import lax
from jax.experimental import pallas as pl
from jax.experimental.pallas import tpu as pltpu
from jax.sharding import Mesh, PartitionSpec as P

HD = 64
TOK_VIEW = 256
X = 4
C = 2
PLANE = 16
LOCAL = 8
LANES = 128
BASE2 = math.log2(math.e) / math.sqrt(HD)
NEG = -1e30
RANGES = ((-2, 2), (0, 1), (1, 2), (-1, 3), (-2, 1), (2, 1))
VMEM_BYTES = 40 << 20


def swap_halves(x):
    return jnp.concatenate([x[:, HD:], x[:, :HD]], axis=1)


def low_lanes(shape):
    return lax.broadcasted_iota(jnp.int32, shape, 1) < HD


def pack_kernel(q_hbm, k_hbm, v_hbm, cam_hbm, out_ref, q_ref, k_ref, v_ref, cam_ref, sems):
    copies = [
        pltpu.make_async_copy(source, target, sems.at[i])
        for i, (source, target) in enumerate(
            [(cam_hbm, cam_ref), (k_hbm, k_ref), (v_hbm, v_ref), (q_hbm, q_ref)]
        )
    ]
    for copy in copies:
        copy.start()
    for copy in copies:
        copy.wait()
    cam = cam_ref[...].astype(jnp.float32)
    low = low_lanes((TOK_VIEW, LANES))
    for pair in range(2):
        cols = slice(pair * LANES, (pair + 1) * LANES)
        queries = []
        for view in range(2):
            rows = slice(view * TOK_VIEW, (view + 1) * TOK_VIEW)
            shift = cam[view : view + 1, cols]
            k = k_ref[rows, cols].astype(jnp.float32) + shift
            v = v_ref[rows, cols].astype(jnp.float32)
            out_ref[2 * pair, rows, :] = jnp.where(low, k, swap_halves(v)).astype(jnp.bfloat16)
            out_ref[2 * pair + 1, rows, :] = jnp.where(low, swap_halves(k), v).astype(jnp.bfloat16)
            queries.append(q_ref[rows, cols].astype(jnp.float32) + shift)
        first, second = queries
        rows = slice(2 * TOK_VIEW, 3 * TOK_VIEW)
        out_ref[2 * pair, rows, :] = jnp.where(low, first, swap_halves(second)).astype(jnp.bfloat16)
        out_ref[2 * pair + 1, rows, :] = jnp.where(low, swap_halves(first), second).astype(
            jnp.bfloat16
        )


def attend_kernel(bounds_hbm, q_ref, *refs, sides, side0, side_step, tile0, q_row, has_state):
    planes = sum(sides)
    kv_hbm = refs[:planes]
    refs = refs[planes:]
    if has_state:
        before, refs = refs[0], refs[1:]
    state, bounds, bounds_sem, q_rows, kv_buf, v_buf, top, kv_sems = refs
    size, rows_tile = LOCAL * TOK_VIEW, 2 * TOK_VIEW
    kv_copies = [
        pltpu.make_async_copy(kv_hbm[p], kv_buf.at[pl.ds(p * size, size), :], kv_sems.at[p])
        for p in range(planes)
    ]
    bounds_copy = pltpu.make_async_copy(bounds_hbm, bounds, bounds_sem)
    bounds_copy.start()
    for copy in kv_copies:
        copy.start()
    lane = lax.broadcasted_iota(jnp.int32, (1, LANES), 1)
    keep = jnp.where(lane < HD, 0.0, 1.0).astype(jnp.bfloat16)
    ones = jnp.where(lane < HD, 1.0, 0.0).astype(jnp.bfloat16)

    def plane_ready(first, end):
        for p in range(first, end):
            kv_copies[p].wait()

        def fill(i, carry):
            part = pl.ds(pl.multiple_of(i * 2 * TOK_VIEW, 2 * TOK_VIEW), 2 * TOK_VIEW)
            v_buf[part, :] = kv_buf[part, :] * keep + ones
            return carry

        lax.fori_loop(first * LOCAL // 2, end * LOCAL // 2, fill, 0)

    for t in range(X):
        packed = q_ref[t, q_row : q_row + TOK_VIEW, :]
        low = low_lanes((TOK_VIEW, LANES))
        zero = jnp.zeros((), jnp.bfloat16)
        row = t * rows_tile
        q_rows[row : row + TOK_VIEW, :] = jnp.where(low, packed, zero)
        q_rows[row + TOK_VIEW : row + rows_tile, :] = jnp.where(low, swap_halves(packed), zero)
        if has_state:
            packed = before[row : row + rows_tile, :]
            state[row : row + rows_tile, :] = packed
            top[row : row + rows_tile, :] = jnp.broadcast_to(packed[:, :1], packed.shape)
        else:
            top[row : row + rows_tile, :] = jnp.full((rows_tile, LANES), NEG, jnp.float32)
            state[row : row + rows_tile, :] = jnp.zeros((rows_tile, LANES), jnp.float32)

    def visit(rows, row0, tiles, start, end):
        def variant(n, key0, row0, tiles, parts):
            keys = pl.ds(pl.multiple_of(key0 * TOK_VIEW, TOK_VIEW), n * TOK_VIEW)

            def step(i, carry):
                def here(part):
                    at = row0 + (i * parts + part) * rows
                    return pl.ds(pl.multiple_of(at, rows), rows)

                def scores(part):
                    return lax.dot_general(
                        q_rows[here(part), :],
                        kv_buf[keys, :],
                        (((1,), (1,)), ((), ())),
                        preferred_element_type=jnp.float32,
                    )

                ahead = scores(0)
                for part in range(parts):
                    s = ahead
                    if part + 1 < parts:
                        ahead = scores(part + 1)
                    piece = here(part)
                    old = top[piece, :]
                    new = jnp.maximum(old, jnp.max(s, axis=1, keepdims=True))
                    shift = jnp.concatenate([new * BASE2] * (2 * n), axis=1)
                    weights = jnp.exp2(s * BASE2 - shift).astype(jnp.bfloat16)
                    factor = jnp.exp2((old - new) * BASE2)
                    update = jnp.dot(weights, v_buf[keys, :], preferred_element_type=jnp.float32)
                    top[piece, :] = new
                    state[piece, :] = state[piece, :] * factor + update
                return carry

            lax.fori_loop(0, tiles, step, 0)

        count = end - start

        def repeat(times, n, row0, tiles, parts):
            def one(c, carry):
                variant(n, start + n * c, row0, tiles, parts)
                return carry

            lax.fori_loop(0, times, one, 0)

        if rows == rows_tile:
            pairs, odd = tiles // 2, tiles % 2
            last = row0 + pairs * 2 * rows
            repeat(jnp.where(pairs > 0, count // 4, 0), 4, row0, pairs, 2)
            repeat(odd * (count // 4), 4, last, 1, 1)
        elif planes > 2:
            repeat(count // 8, 8, row0, tiles, 1)
            pl.when(count % 8 >= 4)(lambda: variant(4, start + count // 8 * 8, row0, tiles, 1))
        else:
            repeat(count // 4, 4, row0, tiles, 1)
        for n in (2, 1):
            key0 = start + (count // (2 * n)) * (2 * n)
            left = count % (2 * n) >= n
            if rows == rows_tile:
                two = jnp.logical_and(left, pairs > 0)
                one = jnp.logical_and(left, odd > 0)
                pl.when(two)(functools.partial(variant, n, key0, row0, pairs, 2))
                pl.when(one)(functools.partial(variant, n, key0, last, 1, 1))
            else:
                pl.when(left)(functools.partial(variant, n, key0, row0, tiles, 1))

    def side(i, carry):
        shift = LOCAL * sides[0] * i
        for j in range(len(sides)):
            ends = sum(sides[: j + 1])
            pl.when(i == j)(functools.partial(plane_ready, ends - sides[j], ends))

        def limits(t, w):
            at = (((side0 + side_step * i) * 2 * X + tile0 + t) * 2 + w) * 2
            return bounds[at] + shift, bounds[at + 1] + shift

        def equal(one, other):
            return jnp.logical_and(one[0] == other[0], one[1] == other[1])

        alike = [equal(limits(t, 0), limits(t, 1)) for t in range(X)]
        joined = [
            jnp.logical_and(
                jnp.logical_and(alike[t - 1], alike[t]), equal(limits(t - 1, 0), limits(t, 0))
            ).astype(jnp.int32)
            for t in range(1, X)
        ]
        run3 = 1
        run2 = 1 + joined[2] * run3
        run1 = 1 + joined[1] * run2
        run0 = 1 + joined[0] * run1

        def tile(t, carry):
            run = jnp.where(t == 0, run0, jnp.where(t == 1, run1, jnp.where(t == 2, run2, run3)))
            inside = jnp.where(
                t == 0,
                0,
                jnp.where(t == 1, joined[0], jnp.where(t == 2, joined[1], joined[2])),
            )
            first, second = limits(t, 0), limits(t, 1)
            whole = equal(first, second)
            row0 = pl.multiple_of(t * rows_tile, rows_tile)

            @pl.when(jnp.logical_and(whole, inside == 0))
            def _():
                visit(rows_tile, row0, run, *first)

            @pl.when(jnp.logical_not(whole))
            def _():
                def one(w, carry):
                    visit(
                        TOK_VIEW,
                        row0 + w * TOK_VIEW,
                        1,
                        jnp.where(w == 0, first[0], second[0]),
                        jnp.where(w == 0, first[1], second[1]),
                    )
                    return carry

                lax.fori_loop(0, 2, one, 0)

            return carry

        lax.fori_loop(0, X, tile, 0)
        return carry

    bounds_copy.wait()
    lax.fori_loop(0, len(sides), side, 0)
    for t in range(X):
        lane = lax.broadcasted_iota(jnp.int32, (rows_tile, LANES), 1)
        row = t * rows_tile
        state[row : row + rows_tile, :] = jnp.where(
            lane < HD // 2, top[row : row + rows_tile, :], state[row : row + rows_tile, :]
        )


def attend(bounds, q, q_row, tile0, kv_planes, sides, side0, side_step, state, name):
    planes = len(kv_planes)
    anywhere = pl.BlockSpec(memory_space=pl.ANY)
    vmem = pl.BlockSpec(memory_space=pltpu.VMEM)
    inputs = [bounds, q, *kv_planes] + ([] if state is None else [state])
    rows = X * 2 * TOK_VIEW
    return pl.pallas_call(
        functools.partial(
            attend_kernel,
            sides=sides,
            side0=side0,
            side_step=side_step,
            tile0=tile0,
            q_row=q_row,
            has_state=state is not None,
        ),
        out_shape=jax.ShapeDtypeStruct((rows, LANES), jnp.float32),
        in_specs=[anywhere, vmem, *[anywhere] * planes, *[vmem] * (state is not None)],
        out_specs=vmem,
        scratch_shapes=[
            pltpu.SMEM(bounds.shape, jnp.int32),
            pltpu.SemaphoreType.DMA(()),
            pltpu.VMEM((rows, LANES), jnp.bfloat16),
            pltpu.VMEM((planes * LOCAL * TOK_VIEW, LANES), jnp.bfloat16),
            pltpu.VMEM((planes * LOCAL * TOK_VIEW, LANES), jnp.bfloat16),
            pltpu.VMEM((rows, LANES), jnp.float32),
            pltpu.SemaphoreType.DMA((planes,)),
        ],
        compiler_params=pltpu.CompilerParams(vmem_limit_bytes=VMEM_BYTES),
        cost_estimate=pl.CostEstimate(
            flops=planes * 2 * rows * (LOCAL * TOK_VIEW) * 2 * TOK_VIEW,
            transcendentals=planes * rows * (LOCAL * TOK_VIEW),
            bytes_accessed=planes << 20,
        ),
        name=name,
    )(*inputs)


def join_kernel(own_ref, got_ref, out_ref):
    rows_tile = 2 * TOK_VIEW
    low = low_lanes((HD, LANES))
    for t in range(X):
        rows = slice(t * rows_tile, (t + 1) * rows_tile)
        a, b = own_ref[rows, :], got_ref[rows, :]
        m_a, m_b = a[:, :1], b[:, :1]
        change = (m_b - m_a) * BASE2
        total = a * jnp.exp2(jnp.minimum(-change, 0.0)) + b * jnp.exp2(jnp.minimum(change, 0.0))
        done = total * (1.0 / total[:, HD // 2 : HD // 2 + 1])
        for i in range(4):
            upper = done[i * LANES : i * LANES + HD]
            lower = done[i * LANES + HD : (i + 1) * LANES]
            out_ref[4 * t + i] = jnp.where(low, swap_halves(upper), lower).astype(jnp.bfloat16)


def project_kernel(y_ref, parts_ref, *refs):
    weights, (out_ref, rows_ref, sum_ref) = refs[:4], refs[4:]
    low = low_lanes((HD, LANES))
    for k in range(4):
        y = (y_ref[0] + 4 - k) % 4
        for pair in range(2):
            a = parts_ref[2 * pair * 4 + y].astype(jnp.float32)
            b = parts_ref[(2 * pair + 1) * 4 + y].astype(jnp.float32)
            cols = slice(pair * LANES, (pair + 1) * LANES)
            rows_ref[k, :HD, cols] = jnp.where(low, a, swap_halves(b)).astype(jnp.bfloat16)
            rows_ref[k, HD:, cols] = jnp.where(low, swap_halves(a), b).astype(jnp.bfloat16)
    for k in range(4):
        part = jnp.dot(rows_ref[k], weights[k][...], preferred_element_type=jnp.float32)
        if k == 0:
            sum_ref[...] = part
        elif k < 3:
            sum_ref[...] += part
        else:
            out_ref[...] = (sum_ref[...] + part).astype(jnp.bfloat16)


def key_ranges(view_object, plane, core):
    tile = jnp.arange(2 * X)
    inner = 4 * (tile % X) + 2 * jnp.where(tile < X, core, 1 - core)
    view = PLANE * plane + inner[:, None] + jnp.arange(2)[None, :]
    own = jnp.sum(
        jnp.where(
            jnp.arange(view_object.shape[0])[None, None, :] == view[:, :, None],
            view_object[None, None, :],
            0,
        ),
        axis=-1,
    )
    first = jnp.sum(view_object[None, None, :] < own[:, :, None], axis=-1)
    end = jnp.sum(view_object[None, None, :] <= own[:, :, None], axis=-1)
    edges = jnp.stack([first, end], axis=-1)
    offset = PLANE * (plane + jnp.array([first for first, _ in RANGES]))
    most = PLANE * jnp.array([count for _, count in RANGES])
    edges = jnp.clip(edges[None] - offset[:, None, None, None], 0, most[:, None, None, None])
    local = 2 * (edges // 4) + jnp.clip(edges % 4 - 2 * core, 0, 2)
    return local.astype(jnp.int32).reshape(-1)


def body(queries, keys, values, camera, view_object, out_weight):
    vmem = pl.BlockSpec(memory_space=pltpu.VMEM)
    z_count = lax.axis_size("z")
    up = [(i, (i + 1) % z_count) for i in range(z_count)]
    down = [(i, (i - 1) % z_count) for i in range(z_count)]
    cores = [(0, 1), (1, 0)]
    plane, core = lax.axis_index("z"), lax.axis_index("c")
    sent = pl.pallas_call(
        pack_kernel,
        out_shape=jax.ShapeDtypeStruct((X, 3 * TOK_VIEW, LANES), jnp.bfloat16),
        in_specs=[pl.BlockSpec(memory_space=pl.ANY)] * 4,
        out_specs=vmem,
        scratch_shapes=[
            *(pltpu.VMEM(x.shape, jnp.bfloat16) for x in (queries, keys, values, camera)),
            pltpu.SemaphoreType.DMA((4,)),
        ],
        compiler_params=pltpu.CompilerParams(vmem_limit_bytes=60 << 20),
        name="pack",
    )(queries, keys, values, camera)
    ours = lax.all_to_all(sent, "x", 0, 0, tiled=True)
    _, view_object = lax.optimization_barrier((sent, view_object))
    bounds = key_ranges(view_object, plane, core)
    kv = ours[:, : 2 * TOK_VIEW].reshape(-1, LANES)
    below = lax.ppermute(kv, "z", up)
    above = lax.ppermute(kv, "z", down)
    q_oth = lax.ppermute(ours[:, 2 * TOK_VIEW :], "c", cores)
    own_row = 2 * TOK_VIEW
    own = attend(bounds, ours, own_row, 0, [kv], (1,), 1, 0, None, "here_own")
    own, sent_weight = lax.optimization_barrier((own, out_weight))
    weights = [out_weight] + [
        lax.ppermute(sent_weight, "y", [(i, (i + k) % 4) for i in range(4)]) for k in (1, 2, 3)
    ]
    below, above, own = lax.optimization_barrier((below, above, own))
    below_far = lax.ppermute(below, "z", up)
    above_far = lax.ppermute(above, "z", down)
    oth = attend(bounds, q_oth, 0, X, [below, kv, above], (3,), 3, 0, None, "near_other")
    oth = attend(bounds, q_oth, 0, X, [below_far, above_far], (1, 1), 4, 1, oth, "far_other")
    got = lax.ppermute(oth, "c", cores)
    rest = [below_far, below, above, above_far]
    own = attend(bounds, ours, own_row, 0, rest, (2, 2), 0, 2, own, "rest_own")
    attended = pl.pallas_call(
        join_kernel,
        out_shape=jax.ShapeDtypeStruct((16, HD, LANES), jnp.bfloat16),
        in_specs=[vmem, vmem],
        out_specs=vmem,
        compiler_params=pltpu.CompilerParams(vmem_limit_bytes=VMEM_BYTES),
        name="join",
    )(own, got)
    parts = lax.all_to_all(attended, ("x", "y"), 0, 0, tiled=True)
    return pl.pallas_call(
        project_kernel,
        out_shape=jax.ShapeDtypeStruct((LANES, 1024), jnp.bfloat16),
        in_specs=[pl.BlockSpec(memory_space=pltpu.SMEM)] + [vmem] * 5,
        out_specs=vmem,
        scratch_shapes=[
            pltpu.VMEM((4, LANES, 256), jnp.bfloat16),
            pltpu.VMEM((LANES, 1024), jnp.float32),
        ],
        compiler_params=pltpu.CompilerParams(vmem_limit_bytes=VMEM_BYTES),
        name="project",
    )(lax.axis_index("y").astype(jnp.int32).reshape(1), parts, *weights)


def solution(mesh):
    views = mesh.shape["obj"] // (X * C)
    grid = Mesh(mesh.devices.reshape(views, X, C, mesh.shape["head"]), ("z", "x", "c", "y"))
    obj = ("z", "x", "c")
    return jax.shard_map(
        body,
        mesh=grid,
        in_specs=(
            P(obj, "y"),
            P(obj, "y"),
            P(obj, "y"),
            P(obj, "y"),
            P(),
            P("y", None),
        ),
        out_specs=P((*obj, "y"), None),
        check_vma=False,
    )
```

```python
import functools
import math

import jax
import jax.numpy as jnp
from jax import lax
from jax.experimental import pallas as pl
from jax.experimental.pallas import tpu as pltpu
from jax.sharding import Mesh, PartitionSpec as P

HD = 64
TOK_VIEW = 256
X = 4
C = 2
PLANE = 16
LOCAL = 8
LANES = 128
BASE2 = math.log2(math.e) / math.sqrt(HD)
NEG = -1e30
RANGES = ((-2, 2), (0, 1), (1, 2), (-1, 3), (-2, 1), (2, 1))
VMEM_BYTES = 40 << 20


def swap_halves(x):
    return jnp.concatenate([x[:, HD:], x[:, :HD]], axis=1)


def low_lanes(shape):
    return lax.broadcasted_iota(jnp.int32, shape, 1) < HD


def pack_kernel(
    q_hbm, k_hbm, v_hbm, cam_hbm, out_hbm, q_ref, k_ref, v_ref, cam_ref, out_ref, sems, out_sems
):
    copies = [
        pltpu.make_async_copy(source, target, sems.at[i])
        for i, (source, target) in enumerate(
            [(cam_hbm, cam_ref), (k_hbm, k_ref), (v_hbm, v_ref), (q_hbm, q_ref)]
        )
    ]
    for copy in copies:
        copy.start()
    for copy in copies:
        copy.wait()
    cam = cam_ref[...].astype(jnp.float32)
    low = low_lanes((TOK_VIEW, LANES))
    leaving = []
    for pair in range(2):
        cols = slice(pair * LANES, (pair + 1) * LANES)
        queries = []
        for view in range(2):
            rows = slice(view * TOK_VIEW, (view + 1) * TOK_VIEW)
            shift = cam[view : view + 1, cols]
            k = k_ref[rows, cols].astype(jnp.float32) + shift
            v = v_ref[rows, cols].astype(jnp.float32)
            out_ref[2 * pair, rows, :] = jnp.where(low, k, swap_halves(v)).astype(jnp.bfloat16)
            out_ref[2 * pair + 1, rows, :] = jnp.where(low, swap_halves(k), v).astype(jnp.bfloat16)
            queries.append(q_ref[rows, cols].astype(jnp.float32) + shift)
        first, second = queries
        rows = slice(2 * TOK_VIEW, 3 * TOK_VIEW)
        out_ref[2 * pair, rows, :] = jnp.where(low, first, swap_halves(second)).astype(jnp.bfloat16)
        out_ref[2 * pair + 1, rows, :] = jnp.where(low, swap_halves(first), second).astype(
            jnp.bfloat16
        )
        heads = pl.ds(2 * pair, 2)
        leaving.append(
            pltpu.make_async_copy(out_ref.at[heads], out_hbm.at[heads], out_sems.at[pair])
        )
        leaving[-1].start()
    for copy in leaving:
        copy.wait()


def attend_kernel(bounds_hbm, q_ref, *refs, sides, side0, side_step, tile0, q_row, has_state):
    planes = sum(sides)
    kv_hbm = refs[:planes]
    refs = refs[planes:]
    if has_state:
        before, refs = refs[0], refs[1:]
    state, bounds, bounds_sem, q_rows, kv_buf, v_buf, top, kv_sems = refs
    size, rows_tile = LOCAL * TOK_VIEW, 2 * TOK_VIEW
    kv_copies = [
        pltpu.make_async_copy(kv_hbm[p], kv_buf.at[pl.ds(p * size, size), :], kv_sems.at[p])
        for p in range(planes)
    ]
    bounds_copy = pltpu.make_async_copy(bounds_hbm, bounds, bounds_sem)
    bounds_copy.start()
    for copy in kv_copies:
        copy.start()
    lane = lax.broadcasted_iota(jnp.int32, (1, LANES), 1)
    keep = jnp.where(lane < HD, 0.0, 1.0).astype(jnp.bfloat16)
    ones = jnp.where(lane < HD, 1.0, 0.0).astype(jnp.bfloat16)

    def plane_ready(first, end):
        for p in range(first, end):
            kv_copies[p].wait()

        def fill(i, carry):
            part = pl.ds(pl.multiple_of(i * 2 * TOK_VIEW, 2 * TOK_VIEW), 2 * TOK_VIEW)
            v_buf[part, :] = kv_buf[part, :] * keep + ones
            return carry

        lax.fori_loop(first * LOCAL // 2, end * LOCAL // 2, fill, 0)

    for t in range(X):
        packed = q_ref[t, q_row : q_row + TOK_VIEW, :]
        low = low_lanes((TOK_VIEW, LANES))
        zero = jnp.zeros((), jnp.bfloat16)
        row = t * rows_tile
        q_rows[row : row + TOK_VIEW, :] = jnp.where(low, packed, zero)
        q_rows[row + TOK_VIEW : row + rows_tile, :] = jnp.where(low, swap_halves(packed), zero)
        if has_state:
            packed = before[row : row + rows_tile, :]
            state[row : row + rows_tile, :] = packed
            top[row : row + rows_tile, :] = jnp.broadcast_to(packed[:, :1], packed.shape)
        else:
            top[row : row + rows_tile, :] = jnp.full((rows_tile, LANES), NEG, jnp.float32)
            state[row : row + rows_tile, :] = jnp.zeros((rows_tile, LANES), jnp.float32)

    def visit(rows, row0, tiles, start, end):
        def variant(n, key0, row0, tiles, parts):
            keys = pl.ds(pl.multiple_of(key0 * TOK_VIEW, TOK_VIEW), n * TOK_VIEW)

            def step(i, carry):
                def here(part):
                    at = row0 + (i * parts + part) * rows
                    return pl.ds(pl.multiple_of(at, rows), rows)

                def scores(part):
                    return lax.dot_general(
                        q_rows[here(part), :],
                        kv_buf[keys, :],
                        (((1,), (1,)), ((), ())),
                        preferred_element_type=jnp.float32,
                    )

                ahead = scores(0)
                for part in range(parts):
                    s = ahead
                    if part + 1 < parts:
                        ahead = scores(part + 1)
                    piece = here(part)
                    old = top[piece, :]
                    new = jnp.maximum(old, jnp.max(s, axis=1, keepdims=True))
                    shift = jnp.concatenate([new * BASE2] * (2 * n), axis=1)
                    weights = jnp.exp2(s * BASE2 - shift).astype(jnp.bfloat16)
                    factor = jnp.exp2((old - new) * BASE2)
                    update = jnp.dot(weights, v_buf[keys, :], preferred_element_type=jnp.float32)
                    top[piece, :] = new
                    state[piece, :] = state[piece, :] * factor + update
                return carry

            lax.fori_loop(0, tiles, step, 0)

        count = end - start

        def repeat(times, n, row0, tiles, parts):
            def one(c, carry):
                variant(n, start + n * c, row0, tiles, parts)
                return carry

            lax.fori_loop(0, times, one, 0)

        if rows == rows_tile:
            pairs, odd = tiles // 2, tiles % 2
            last = row0 + pairs * 2 * rows
            repeat(jnp.where(pairs > 0, count // 4, 0), 4, row0, pairs, 2)
            repeat(odd * (count // 4), 4, last, 1, 1)
        elif planes > 2:
            repeat(count // 8, 8, row0, tiles, 1)
            pl.when(count % 8 >= 4)(lambda: variant(4, start + count // 8 * 8, row0, tiles, 1))
        else:
            repeat(count // 4, 4, row0, tiles, 1)
        for n in (2, 1):
            key0 = start + (count // (2 * n)) * (2 * n)
            left = count % (2 * n) >= n
            if rows == rows_tile:
                two = jnp.logical_and(left, pairs > 0)
                one = jnp.logical_and(left, odd > 0)
                pl.when(two)(functools.partial(variant, n, key0, row0, pairs, 2))
                pl.when(one)(functools.partial(variant, n, key0, last, 1, 1))
            else:
                pl.when(left)(functools.partial(variant, n, key0, row0, tiles, 1))

    def side(i, carry):
        shift = LOCAL * sides[0] * i
        for j in range(len(sides)):
            ends = sum(sides[: j + 1])
            pl.when(i == j)(functools.partial(plane_ready, ends - sides[j], ends))

        def limits(t, w):
            at = (((side0 + side_step * i) * 2 * X + tile0 + t) * 2 + w) * 2
            return bounds[at] + shift, bounds[at + 1] + shift

        def equal(one, other):
            return jnp.logical_and(one[0] == other[0], one[1] == other[1])

        alike = [equal(limits(t, 0), limits(t, 1)) for t in range(X)]
        joined = [
            jnp.logical_and(
                jnp.logical_and(alike[t - 1], alike[t]), equal(limits(t - 1, 0), limits(t, 0))
            ).astype(jnp.int32)
            for t in range(1, X)
        ]
        run3 = 1
        run2 = 1 + joined[2] * run3
        run1 = 1 + joined[1] * run2
        run0 = 1 + joined[0] * run1

        def tile(t, carry):
            run = jnp.where(t == 0, run0, jnp.where(t == 1, run1, jnp.where(t == 2, run2, run3)))
            inside = jnp.where(
                t == 0,
                0,
                jnp.where(t == 1, joined[0], jnp.where(t == 2, joined[1], joined[2])),
            )
            first, second = limits(t, 0), limits(t, 1)
            whole = equal(first, second)
            row0 = pl.multiple_of(t * rows_tile, rows_tile)

            @pl.when(jnp.logical_and(whole, inside == 0))
            def _():
                visit(rows_tile, row0, run, *first)

            @pl.when(jnp.logical_not(whole))
            def _():
                def one(w, carry):
                    visit(
                        TOK_VIEW,
                        row0 + w * TOK_VIEW,
                        1,
                        jnp.where(w == 0, first[0], second[0]),
                        jnp.where(w == 0, first[1], second[1]),
                    )
                    return carry

                lax.fori_loop(0, 2, one, 0)

            return carry

        lax.fori_loop(0, X, tile, 0)
        return carry

    bounds_copy.wait()
    lax.fori_loop(0, len(sides), side, 0)
    for t in range(X):
        lane = lax.broadcasted_iota(jnp.int32, (rows_tile, LANES), 1)
        row = t * rows_tile
        state[row : row + rows_tile, :] = jnp.where(
            lane < HD // 2, top[row : row + rows_tile, :], state[row : row + rows_tile, :]
        )


def attend(bounds, q, q_row, tile0, kv_planes, sides, side0, side_step, state, name):
    planes = len(kv_planes)
    anywhere = pl.BlockSpec(memory_space=pl.ANY)
    vmem = pl.BlockSpec(memory_space=pltpu.VMEM)
    inputs = [bounds, q, *kv_planes] + ([] if state is None else [state])
    rows = X * 2 * TOK_VIEW
    return pl.pallas_call(
        functools.partial(
            attend_kernel,
            sides=sides,
            side0=side0,
            side_step=side_step,
            tile0=tile0,
            q_row=q_row,
            has_state=state is not None,
        ),
        out_shape=jax.ShapeDtypeStruct((rows, LANES), jnp.float32),
        in_specs=[anywhere, vmem, *[anywhere] * planes, *[vmem] * (state is not None)],
        out_specs=vmem,
        scratch_shapes=[
            pltpu.SMEM(bounds.shape, jnp.int32),
            pltpu.SemaphoreType.DMA(()),
            pltpu.VMEM((rows, LANES), jnp.bfloat16),
            pltpu.VMEM((planes * LOCAL * TOK_VIEW, LANES), jnp.bfloat16),
            pltpu.VMEM((planes * LOCAL * TOK_VIEW, LANES), jnp.bfloat16),
            pltpu.VMEM((rows, LANES), jnp.float32),
            pltpu.SemaphoreType.DMA((planes,)),
        ],
        compiler_params=pltpu.CompilerParams(vmem_limit_bytes=VMEM_BYTES),
        cost_estimate=pl.CostEstimate(
            flops=planes * 2 * rows * (LOCAL * TOK_VIEW) * 2 * TOK_VIEW,
            transcendentals=planes * rows * (LOCAL * TOK_VIEW),
            bytes_accessed=planes << 20,
        ),
        name=name,
    )(*inputs)


def join_kernel(own_ref, got_ref, out_ref):
    rows_tile = 2 * TOK_VIEW
    low = low_lanes((HD, LANES))
    for t in range(X):
        rows = slice(t * rows_tile, (t + 1) * rows_tile)
        a, b = own_ref[rows, :], got_ref[rows, :]
        m_a, m_b = a[:, :1], b[:, :1]
        change = (m_b - m_a) * BASE2
        total = a * jnp.exp2(jnp.minimum(-change, 0.0)) + b * jnp.exp2(jnp.minimum(change, 0.0))
        done = total * (1.0 / total[:, HD // 2 : HD // 2 + 1])
        for i in range(4):
            upper = done[i * LANES : i * LANES + HD]
            lower = done[i * LANES + HD : (i + 1) * LANES]
            out_ref[4 * t + i] = jnp.where(low, swap_halves(upper), lower).astype(jnp.bfloat16)


def project_kernel(y_ref, parts_ref, *refs):
    weights, (out_ref, rows_ref, sum_ref) = refs[:4], refs[4:]
    low = low_lanes((HD, LANES))
    for k in range(4):
        y = (y_ref[0] + 4 - k) % 4
        for pair in range(2):
            a = parts_ref[2 * pair * 4 + y].astype(jnp.float32)
            b = parts_ref[(2 * pair + 1) * 4 + y].astype(jnp.float32)
            cols = slice(pair * LANES, (pair + 1) * LANES)
            rows_ref[k, :HD, cols] = jnp.where(low, a, swap_halves(b)).astype(jnp.bfloat16)
            rows_ref[k, HD:, cols] = jnp.where(low, swap_halves(a), b).astype(jnp.bfloat16)
    for k in range(4):
        part = jnp.dot(rows_ref[k], weights[k][...], preferred_element_type=jnp.float32)
        if k == 0:
            sum_ref[...] = part
        elif k < 3:
            sum_ref[...] += part
        else:
            out_ref[...] = (sum_ref[...] + part).astype(jnp.bfloat16)


def key_ranges(view_object, plane, core):
    tile = jnp.arange(2 * X)
    inner = 4 * (tile % X) + 2 * jnp.where(tile < X, core, 1 - core)
    view = PLANE * plane + inner[:, None] + jnp.arange(2)[None, :]
    own = jnp.sum(
        jnp.where(
            jnp.arange(view_object.shape[0])[None, None, :] == view[:, :, None],
            view_object[None, None, :],
            0,
        ),
        axis=-1,
    )
    first = jnp.sum(view_object[None, None, :] < own[:, :, None], axis=-1)
    end = jnp.sum(view_object[None, None, :] <= own[:, :, None], axis=-1)
    edges = jnp.stack([first, end], axis=-1)
    offset = PLANE * (plane + jnp.array([first for first, _ in RANGES]))
    most = PLANE * jnp.array([count for _, count in RANGES])
    edges = jnp.clip(edges[None] - offset[:, None, None, None], 0, most[:, None, None, None])
    local = 2 * (edges // 4) + jnp.clip(edges % 4 - 2 * core, 0, 2)
    return local.astype(jnp.int32).reshape(-1)


def body(queries, keys, values, camera, view_object, out_weight):
    vmem = pl.BlockSpec(memory_space=pltpu.VMEM)
    z_count = lax.axis_size("z")
    up = [(i, (i + 1) % z_count) for i in range(z_count)]
    down = [(i, (i - 1) % z_count) for i in range(z_count)]
    cores = [(0, 1), (1, 0)]
    plane, core = lax.axis_index("z"), lax.axis_index("c")
    sent = pl.pallas_call(
        pack_kernel,
        out_shape=jax.ShapeDtypeStruct((X, 3 * TOK_VIEW, LANES), jnp.bfloat16),
        in_specs=[pl.BlockSpec(memory_space=pl.ANY)] * 4,
        out_specs=pl.BlockSpec(memory_space=pl.ANY),
        scratch_shapes=[
            *(pltpu.VMEM(x.shape, jnp.bfloat16) for x in (queries, keys, values, camera)),
            pltpu.VMEM((X, 3 * TOK_VIEW, LANES), jnp.bfloat16),
            pltpu.SemaphoreType.DMA((4,)),
            pltpu.SemaphoreType.DMA((2,)),
        ],
        compiler_params=pltpu.CompilerParams(vmem_limit_bytes=60 << 20),
        name="pack",
    )(queries, keys, values, camera)
    ours = lax.all_to_all(sent, "x", 0, 0, tiled=True)
    _, view_object = lax.optimization_barrier((sent, view_object))
    bounds = key_ranges(view_object, plane, core)
    kv = ours[:, : 2 * TOK_VIEW].reshape(-1, LANES)
    below = lax.ppermute(kv, "z", up)
    above = lax.ppermute(kv, "z", down)
    q_oth = lax.ppermute(ours[:, 2 * TOK_VIEW :], "c", cores)
    own_row = 2 * TOK_VIEW
    own = attend(bounds, ours, own_row, 0, [kv], (1,), 1, 0, None, "here_own")
    own, sent_weight = lax.optimization_barrier((own, out_weight))
    weights = [out_weight] + [
        lax.ppermute(sent_weight, "y", [(i, (i + k) % 4) for i in range(4)]) for k in (1, 2, 3)
    ]
    below, above, own = lax.optimization_barrier((below, above, own))
    below_far = lax.ppermute(below, "z", up)
    above_far = lax.ppermute(above, "z", down)
    oth = attend(bounds, q_oth, 0, X, [below, kv, above], (3,), 3, 0, None, "near_other")
    oth = attend(bounds, q_oth, 0, X, [below_far, above_far], (1, 1), 4, 1, oth, "far_other")
    got = lax.ppermute(oth, "c", cores)
    rest = [below_far, below, above, above_far]
    own = attend(bounds, ours, own_row, 0, rest, (2, 2), 0, 2, own, "rest_own")
    attended = pl.pallas_call(
        join_kernel,
        out_shape=jax.ShapeDtypeStruct((16, HD, LANES), jnp.bfloat16),
        in_specs=[vmem, vmem],
        out_specs=vmem,
        compiler_params=pltpu.CompilerParams(vmem_limit_bytes=VMEM_BYTES),
        name="join",
    )(own, got)
    parts = lax.all_to_all(attended, ("x", "y"), 0, 0, tiled=True)
    return pl.pallas_call(
        project_kernel,
        out_shape=jax.ShapeDtypeStruct((LANES, 1024), jnp.bfloat16),
        in_specs=[pl.BlockSpec(memory_space=pltpu.SMEM)] + [vmem] * 5,
        out_specs=vmem,
        scratch_shapes=[
            pltpu.VMEM((4, LANES, 256), jnp.bfloat16),
            pltpu.VMEM((LANES, 1024), jnp.float32),
        ],
        compiler_params=pltpu.CompilerParams(vmem_limit_bytes=VMEM_BYTES),
        name="project",
    )(lax.axis_index("y").astype(jnp.int32).reshape(1), parts, *weights)


def solution(mesh):
    views = mesh.shape["obj"] // (X * C)
    grid = Mesh(mesh.devices.reshape(views, X, C, mesh.shape["head"]), ("z", "x", "c", "y"))
    obj = ("z", "x", "c")
    return jax.shard_map(
        body,
        mesh=grid,
        in_specs=(
            P(obj, "y"),
            P(obj, "y"),
            P(obj, "y"),
            P(obj, "y"),
            P(),
            P("y", None),
        ),
        out_specs=P((*obj, "y"), None),
        check_vma=False,
    )
```
